256 devices in a mesh: ctx: 32 (over x, z), dp: 2 (over core), tp: 4 (over y).
Axes of the slice: x: 4, y: 4, z: 8, core: 2. Of those that a mesh axis runs over, the one named last changes fastest.
Arguments:
- ssm_input: bfloat16 [2, 4096, 8192], P('dp', 'ctx', 'tp'), may hold values from -12 to 12
- ssm_gate: bfloat16 [2, 4096, 8192], P('dp', 'ctx', 'tp'), may hold values from -5 to 5
- step_raw: float32 [2, 128, 4096], P('dp', 'tp', 'ctx'), may hold values from -6 to 0
- b_proj: bfloat16 [2, 4096, 1024], P('dp', 'ctx', 'tp'), may hold values from -1.796875 to 1.796875
- c_proj: bfloat16 [2, 4096, 1024], P('dp', 'ctx', 'tp'), may hold values from -1.796875 to 1.796875
- rate_log: float32 [128], P('tp'), may hold values from -25 to 0
- step_bias: float32 [128], P('tp'), may hold values from -0.5 to 0.5
- skip_gain: float32 [128], P('tp'), may hold values from 0.5 to 1.5
- norm_gain: float32 [8192], P('tp'), may hold values from 0.25 to 1.75
- ssm_grad_out: bfloat16 [2, 4096, 8192], P('dp', 'ctx', 'tp'), may hold values from -6 to 6
- queries: bfloat16 [2, 4096, 8192], P('dp', 'ctx', 'tp'), may hold values from -24 to 24
- keys: bfloat16 [2, 4096, 1024], P('dp', 'ctx', 'tp'), may hold values from -4 to 4
- values: bfloat16 [2, 4096, 1024], P('dp', 'ctx', 'tp'), may hold values from -6 to 6
- attention_output_gradient: bfloat16 [2, 4096, 8192], P('dp', 'ctx', 'tp'), may hold values from -6 to 6
- doc_lengths: int32 [2, 17], P('dp'), may hold values from 1 to 512, 4096 in all within a row
Outputs:
- grad_input: bfloat16 [2, 4096, 8192], P('dp', 'ctx', 'tp')
- grad_gate: bfloat16 [2, 4096, 8192], P('dp', 'ctx', 'tp')
- grad_raw: float32 [2, 128, 4096], P('dp', 'tp', 'ctx')
- grad_b: bfloat16 [2, 4096, 1024], P('dp', 'ctx', 'tp')
- grad_c: bfloat16 [2, 4096, 1024], P('dp', 'ctx', 'tp')
- grad_rate: float32 [128], P('tp')
- grad_skip: float32 [128], P('tp')
- grad_gain: float32 [8192], P('tp')
- grad_queries: bfloat16 [2, 4096, 8192], P('dp', 'ctx', 'tp')
- grad_keys: bfloat16 [2, 4096, 1024], P('dp', 'ctx', 'tp')
- grad_values: bfloat16 [2, 4096, 1024], P('dp', 'ctx', 'tp')
The draws below stay inside these ranges and needn't reach their ends.
Inputs may be any that keep to these rules, and one draw needn't show every extreme that they name: `doc_lengths`: each row sums to 4096, and its largest entry is exactly 512.
All inputs are finite; a program needn't handle non-finite values.
Results may differ from the reference program's by a relative error of at most 0.007.
Values may be sent and summed in bfloat16 or wider, within the bound.
A program may use at most 128 MiB of HBM per device.

```python
import math
import jax
import jax.numpy as jnp
import numpy as np
from jax import lax

HS = 128
P_SIZE = 64
NST = 128
G = 8
CH = 128
QUERY_HEADS = 64
KEY_VALUE_HEADS = 8
HEAD_CHANNELS = 128
KEYS_PER_BLOCK = 512
PACKED_SEQUENCES = 2
SEQUENCE_TOKENS = 4096
MOST = 512
DOCS = 17


def draw_ssm_input(key, part):
    base_key = jax.random.fold_in(key, 3)
    shape_all = (PACKED_SEQUENCES, SEQUENCE_TOKENS, HS * P_SIZE)
    head_of = jnp.arange(HS * P_SIZE) // P_SIZE
    exponent_share = head_of.astype(jnp.float32) / (2.0 * max(HS - 1, 1))
    values_drawn = jnp.clip(jax.random.normal(base_key, shape_all, jnp.float32), -5.0, 5.0)
    spread = jnp.power(5.0, exponent_share)
    return (values_drawn * spread[None, None, :]).astype(jnp.bfloat16)


def draw_rate_log(key, part):
    first_key, second_key, third_key = jax.random.split(jax.random.fold_in(key, 5), 3)
    is_slow = jax.random.bernoulli(first_key, 0.5, (HS,))
    fast_rate = jnp.exp(jax.random.uniform(second_key, (HS,), jnp.float32, math.log(0.15), math.log(0.26)))
    slow_rate = jnp.exp(jax.random.uniform(third_key, (HS,), jnp.float32, math.log(0.3), math.log(2.0))) / (0.13 * SEQUENCE_TOKENS)
    return jnp.log(jnp.where(is_slow, slow_rate, fast_rate)).astype(jnp.float32)


def draw_step_raw(key, part):
    base_key = jax.random.fold_in(key, 7)
    shape_all = (PACKED_SEQUENCES, HS, SEQUENCE_TOKENS)
    drawn = -2.0 + 0.5 * jnp.clip(jax.random.normal(base_key, shape_all, jnp.float32), -4.0, 4.0)
    return drawn.astype(jnp.float32)


def drawn_pair(key):
    base_key = jax.random.fold_in(key, 11)
    query_key, pair_key = jax.random.split(base_key, 2)
    shape_query = (PACKED_SEQUENCES, SEQUENCE_TOKENS, QUERY_HEADS * HEAD_CHANNELS)
    paired_shapes = (PACKED_SEQUENCES, SEQUENCE_TOKENS, KEY_VALUE_HEADS * HEAD_CHANNELS)
    sampled_queries = jnp.clip(jax.random.normal(query_key, shape_query, jnp.float32), -4.0, 4.0)
    sampled_keys = jnp.clip(jax.random.normal(pair_key, paired_shapes, jnp.float32), -4.0, 4.0)
    return (sampled_queries, sampled_keys)


def draw_queries(key, part):
    return drawn_pair(key)[0].astype(jnp.bfloat16)


def draw_keys(key, part):
    return drawn_pair(key)[1].astype(jnp.bfloat16)


def steps_of(rng, extent, shards, low, high):
    level, own = 1.0, jax.random.fold_in(rng, 6)
    for dim, shards_of in shards:
        draws = jnp.exp(jax.random.uniform(jax.random.fold_in(own, dim), (shards_of,), jnp.float32, low / len(shards), high / len(shards)))
        level = level * jnp.repeat(draws, extent[dim] // shards_of).reshape([-1 if axis == dim else 1 for axis in range(len(extent))])
    return level


def split_up(count, total, limit, skew):
    portions = [(1 << 20) // math.isqrt(rank ** skew) + 1 for rank in range(2, count + 1)]
    rest, counts = total - limit - (count - 1), [1] * (count - 1)
    while rest > 0:
        movable = [i for i in range(count - 1) if counts[i] < limit]
        pool, remaining = sum([portions[i] for i in movable]), rest
        for i in movable:
            more = min(limit - counts[i], max(1, remaining * portions[i] // pool), rest)
            counts[i] = counts[i] + more
            rest = rest - more
    return np.array([limit] + counts)


def ragged(stream_key, amount, total, limit, skew):
    if amount == 2:
        one = jax.random.randint(stream_key, (), max(1, total - limit), min(limit, total - 1) + 1)
        return jnp.stack([one, total - one])
    sizes = jnp.asarray(split_up(amount, total, limit, skew), jnp.int32)
    couples = (amount - 1) // 2
    giver, receiver = sizes[1:1 + 2 * couples:2], sizes[2:2 + 2 * couples:2]
    margin = jnp.minimum(giver - 1, limit - receiver)
    shifted = jax.random.randint(jax.random.fold_in(stream_key, 1), (couples,), 0, 1 << 20) % (margin + 1)
    sizes = sizes.at[1:1 + 2 * couples:2].set(giver - shifted).at[2:2 + 2 * couples:2].set(receiver + shifted)
    return sizes[jax.random.permutation(jax.random.fold_in(stream_key, 2), amount)]


def bell_draw(rng, dims, deviation, bound, shards=(), kind=jnp.bfloat16):
    values = deviation * jax.random.normal(rng, dims, jnp.float32)
    if shards:
        values = values * steps_of(rng, dims, shards, -0.22, 0.18)
    return jnp.clip(values, -bound, bound).astype(kind)


def setup_inputs(seed: int = 0) -> dict:
    splits = jax.random.split(jax.random.key(seed), 16)
    return {
        "ssm_input": draw_ssm_input(jax.random.fold_in(splits[15], 71), 0),
        "ssm_gate": bell_draw(splits[1], (PACKED_SEQUENCES, SEQUENCE_TOKENS, HS * P_SIZE), 1.0, 5.0, ((0, 2), (1, 32), (2, 4))),
        "step_raw": draw_step_raw(jax.random.fold_in(splits[15], 71), 0),
        "b_proj": bell_draw(splits[3], (PACKED_SEQUENCES, SEQUENCE_TOKENS, G * NST), 0.3, 1.796875, ((0, 2), (1, 32), (2, 4))),
        "c_proj": bell_draw(splits[4], (PACKED_SEQUENCES, SEQUENCE_TOKENS, G * NST), 0.3, 1.796875, ((0, 2), (1, 32), (2, 4))),
        "rate_log": draw_rate_log(jax.random.fold_in(splits[15], 71), 0),
        "step_bias": jnp.clip(jax.random.uniform(splits[6], (HS,), jnp.float32, -0.5, 0.5) * steps_of(splits[6], (HS,), ((0, 4),), -0.4, 0.0), -0.5, 0.5),
        "skip_gain": jnp.clip(0.5 + 1.0 * jax.random.uniform(splits[7], (HS,), jnp.float32) ** steps_of(splits[7], (HS,), ((0, 4),), -0.2, 0.2), 0.5, 1.5),
        "norm_gain": jnp.clip(1.0 + 0.15 * jax.random.normal(splits[8], (HS * P_SIZE,), jnp.float32), 0.25, 1.75),
        "ssm_grad_out": bell_draw(splits[9], (PACKED_SEQUENCES, SEQUENCE_TOKENS, HS * P_SIZE), 1.0, 6.0, ((0, 2), (1, 32), (2, 4))),
        "queries": draw_queries(jax.random.fold_in(splits[15], 71), 0),
        "keys": draw_keys(jax.random.fold_in(splits[15], 71), 0),
        "values": bell_draw(splits[12], (PACKED_SEQUENCES, SEQUENCE_TOKENS, KEY_VALUE_HEADS * HEAD_CHANNELS), 1.0, 6.0, ((0, 2), (1, 32), (2, 4))),
        "attention_output_gradient": bell_draw(splits[13], (PACKED_SEQUENCES, SEQUENCE_TOKENS, QUERY_HEADS * HEAD_CHANNELS), 1.0, 6.0, ((0, 2), (1, 32), (2, 4))),
        "doc_lengths": jax.vmap(lambda own: ragged(own, DOCS, SEQUENCE_TOKENS, MOST, 2))(jax.random.split(splits[14], PACKED_SEQUENCES)).reshape((PACKED_SEQUENCES, DOCS)).astype(jnp.int32),
    }


precise = lax.Precision.HIGHEST
masked_score = -1e+30
norm_epsilon = 1e-05

def doc_index(token_positions, doc_ends):
    return lax.optimization_barrier(jnp.sum((token_positions[:, None] >= doc_ends[None, :]).astype(jnp.int32), axis=1)).astype(jnp.int32)

def doc_begin(token_positions, doc_ends, lengths):
    return lax.optimization_barrier(jnp.sum(jnp.where(token_positions[:, None] >= doc_ends[None, :], lengths[None, :], 0), axis=1)).astype(jnp.int32)

def state_scan(inputs, step_sizes, b_rows, c_rows, decay_rates, skip_gains, document_labels, before, block_len):
    rows_count, head_count, head_width = inputs.shape
    group_count, state_width = (b_rows.shape[1], b_rows.shape[2])
    group_heads = head_count // group_count
    block_count = rows_count // block_len
    x_blocks = inputs.reshape(block_count, block_len, group_count, group_heads, head_width)
    step_blocks = step_sizes.reshape(head_count, block_count, block_len).transpose(1, 0, 2)
    b_blocks = b_rows.reshape(block_count, block_len, group_count, state_width)
    c_blocks = c_rows.reshape(block_count, block_len, group_count, state_width)
    doc_blocks = document_labels.reshape(block_count, block_len)
    offsets = jnp.arange(block_len)
    causal = offsets[:, None] >= offsets[None, :]

    def advance(carried_in, inputs_now):
        state_now, last_doc = carried_in
        x_here, step_here, b_here, c_here, doc_here = inputs_now
        cumulative = jnp.cumsum(-decay_rates[:, None] * step_here, axis=1)
        within = (doc_here[:, None] == doc_here[None, :]) & causal
        exponent = jnp.where(within[None], cumulative[:, :, None] - cumulative[:, None, :], masked_score)
        decays = jnp.exp(exponent).reshape(group_count, group_heads, block_len, block_len)
        intersection = jnp.einsum('tgn,sgn->gts', c_here, b_here, precision=precise)
        weights = decays * intersection[:, None] * step_here.reshape(group_count, group_heads, 1, block_len)
        inside = jnp.einsum('gjts,sgjp->tgjp', weights, x_here, precision=precise)
        survive = jnp.where((doc_here == last_doc)[None, :], jnp.exp(cumulative), 0.0)
        survive = survive.reshape(group_count, group_heads, block_len).transpose(2, 0, 1)
        carried = jnp.einsum('gjpn,tgn->tgjp', state_now, c_here, precision=precise) * survive[..., None]
        outputs = inside + carried + skip_gains.reshape(group_count, group_heads)[None, :, :, None] * x_here
        tail_weight = jnp.where((doc_here == doc_here[-1])[None, :], jnp.exp(cumulative[:, -1:] - cumulative), 0.0) * step_here
        injected = jnp.einsum('gjs,sgjp,sgn->gjpn', tail_weight.reshape(group_count, group_heads, block_len), x_here, b_here, precision=precise)
        retained = jnp.where(doc_here[-1] == last_doc, jnp.exp(cumulative[:, -1]), 0.0).reshape(group_count, group_heads)
        return ((injected + retained[:, :, None, None] * state_now, doc_here[-1]), outputs)
    initial = (jnp.zeros((group_count, group_heads, head_width, state_width), jnp.float32), before)
    (final_state, _), outputs = lax.scan(jax.checkpoint(advance), initial, (x_blocks, step_blocks, b_blocks, c_blocks, doc_blocks))
    return (outputs.reshape(rows_count, head_count, head_width), final_state.reshape(head_count, head_width, state_width))

def attention_grads(query_row_block, grad_rows, key_value_rows, query_pos, query_docs, query_begin, key_pos, key_docs):
    scale_factor = 1.0 / math.sqrt(HEAD_CHANNELS)
    key_count = key_value_rows.shape[0]
    kv_heads = key_value_rows.shape[2]
    heads_per_group = query_row_block.shape[2]
    rows_count = query_row_block.shape[0]
    block_count = key_count // KEYS_PER_BLOCK
    kv_blocks = key_value_rows.reshape(block_count, KEYS_PER_BLOCK, 2, kv_heads, HEAD_CHANNELS)
    pos_blocks = key_pos.reshape(block_count, KEYS_PER_BLOCK)
    doc_blocks = key_docs.reshape(block_count, KEYS_PER_BLOCK)
    lowest = jnp.min(query_begin)
    highest = jnp.max(query_pos)

    def allowed_of(block_pos, block_docs):
        allowed = (block_pos[None, :] <= query_pos[:, None]) & (block_docs[None, :] == query_docs[:, None]) & (block_pos[None, :] >= 0)
        return allowed[None, None]

    def active(block_pos):
        return (block_pos[-1] >= lowest) & (block_pos[0] <= highest)

    def scores_of(block_keys, allowed):
        raw_scores = jnp.einsum('icge,jce->cgij', query_row_block, block_keys, preferred_element_type=jnp.float32) * scale_factor
        return jnp.where(allowed, raw_scores, masked_score)

    def first_pass(running, blocks_now):
        block_kv, block_pos, block_docs = blocks_now

        def accumulate(running):
            top_score, total, weighted = running
            allowed = allowed_of(block_pos, block_docs)
            scores = scores_of(block_kv[:, 0], allowed)
            new_top = jnp.maximum(top_score, lax.optimization_barrier(jnp.max(scores, axis=-1)))
            expo = jnp.where(allowed, jnp.exp(scores - new_top[..., None]), 0.0)
            grad_dots = jnp.einsum('icge,jce->cgij', grad_rows, block_kv[:, 1], preferred_element_type=jnp.float32)
            fade = jnp.exp(top_score - new_top)
            return (new_top, total * fade + lax.optimization_barrier(jnp.sum(expo, axis=-1)), weighted * fade + lax.optimization_barrier(jnp.sum(expo * grad_dots, axis=-1)))

        def unchanged(running):
            return running
        return (lax.cond(active(block_pos), accumulate, unchanged, running), None)
    stat_shape = (kv_heads, heads_per_group, rows_count)
    initial = (jnp.full(stat_shape, masked_score, jnp.float32), jnp.zeros(stat_shape, jnp.float32), jnp.zeros(stat_shape, jnp.float32))
    (top_score, total, weighted), _ = lax.scan(first_pass, initial, (kv_blocks, pos_blocks, doc_blocks))
    log_total = top_score + jnp.log(total)
    centre = weighted / total

    def second_pass(query_gradient, blocks_now):
        block_kv, block_pos, block_docs = blocks_now

        def accumulate(query_gradient):
            allowed = allowed_of(block_pos, block_docs)
            scores = scores_of(block_kv[:, 0], allowed)
            probs = jnp.where(allowed, jnp.exp(scores - log_total[..., None]), 0.0)
            grad_dots = jnp.einsum('icge,jce->cgij', grad_rows, block_kv[:, 1], preferred_element_type=jnp.float32)
            prob_low = probs.astype(jnp.bfloat16)
            score_grad = (probs * (grad_dots - centre[..., None])).astype(jnp.bfloat16)
            grad_key = jnp.einsum('cgij,icge->jce', score_grad, query_row_block, preferred_element_type=jnp.float32) * scale_factor
            grad_value = jnp.einsum('cgij,icge->jce', prob_low, grad_rows, preferred_element_type=jnp.float32)
            query_gradient = query_gradient + jnp.einsum('cgij,jce->icge', score_grad, block_kv[:, 0], preferred_element_type=jnp.float32)
            return (query_gradient, jnp.stack([grad_key, grad_value], axis=1))

        def skipped(query_gradient):
            return (query_gradient, jnp.zeros((KEYS_PER_BLOCK, 2, kv_heads, HEAD_CHANNELS), jnp.float32))
        return lax.cond(active(block_pos), accumulate, skipped, query_gradient)
    query_gradient, gradient_blocks = lax.scan(second_pass, jnp.zeros((rows_count, kv_heads, heads_per_group, HEAD_CHANNELS), jnp.float32), (kv_blocks, pos_blocks, doc_blocks))
    return (query_gradient * scale_factor, gradient_blocks.reshape(key_count, 2, kv_heads, HEAD_CHANNELS))

def mixer_output(inputs, gate_values, raw_steps, b_rows, c_rows, rate_log, step_bias, skip_gain, norm_gain, document_labels):
    step_sizes = jax.nn.softplus(raw_steps + step_bias[:, None])
    decay_rates = jnp.exp(rate_log)
    rows_count = inputs.shape[0]
    head_count = decay_rates.shape[0]
    mixed, _ = state_scan(inputs.reshape(rows_count, head_count, P_SIZE), step_sizes, b_rows.reshape(rows_count, -1, NST), c_rows.reshape(rows_count, -1, NST), decay_rates, skip_gain, document_labels, jnp.array(-1, jnp.int32), CH)
    mixed = mixed.reshape(rows_count, head_count * P_SIZE)
    gated = mixed * (gate_values * jax.nn.sigmoid(gate_values))
    factor = lax.rsqrt(lax.optimization_barrier(jnp.mean(gated * gated, axis=1, keepdims=True)) + norm_epsilon)
    return gated * factor * norm_gain[None, :]

def reference(ssm_input, ssm_gate, step_raw, b_proj, c_proj, rate_log, step_bias, skip_gain, norm_gain, ssm_grad_out, queries, keys, values, attention_output_gradient, doc_lengths):
    token_positions = jnp.arange(SEQUENCE_TOKENS, dtype=jnp.int32)
    all_ends = jnp.cumsum(doc_lengths, axis=1).astype(jnp.int32)
    all_docs = [doc_index(token_positions, all_ends[packed_sequence]) for packed_sequence in range(PACKED_SEQUENCES)]

    def forward(inputs, gates, raw_steps, b_rows, c_rows, rate_log, step_bias, skip_gain, norm_gain):
        results = []
        for packed_sequence in range(PACKED_SEQUENCES):
            results.append(mixer_output(inputs[packed_sequence], gates[packed_sequence], raw_steps[packed_sequence], b_rows[packed_sequence], c_rows[packed_sequence], rate_log, step_bias, skip_gain, norm_gain, all_docs[packed_sequence]))
        return jnp.stack(results)
    _, pull_back = jax.vjp(forward, ssm_input.astype(jnp.float32), ssm_gate.astype(jnp.float32), step_raw, b_proj.astype(jnp.float32), c_proj.astype(jnp.float32), rate_log, step_bias, skip_gain, norm_gain)
    grads = pull_back(ssm_grad_out.astype(jnp.float32))
    heads_per_group = QUERY_HEADS // KEY_VALUE_HEADS
    total_blocks = SEQUENCE_TOKENS // KEYS_PER_BLOCK
    query_list = []
    key_collection = []
    value_collection = []
    for packed_sequence in range(PACKED_SEQUENCES):
        document_labels = all_docs[packed_sequence]
        start_offsets = doc_begin(token_positions, all_ends[packed_sequence], doc_lengths[packed_sequence])
        key_value_rows = jnp.stack([keys[packed_sequence].reshape(SEQUENCE_TOKENS, KEY_VALUE_HEADS, HEAD_CHANNELS), values[packed_sequence].reshape(SEQUENCE_TOKENS, KEY_VALUE_HEADS, HEAD_CHANNELS)], axis=1)
        query_block_list = queries[packed_sequence].reshape(total_blocks, KEYS_PER_BLOCK, KEY_VALUE_HEADS, heads_per_group, HEAD_CHANNELS)
        gradient_blocks = attention_output_gradient[packed_sequence].reshape(total_blocks, KEYS_PER_BLOCK, KEY_VALUE_HEADS, heads_per_group, HEAD_CHANNELS)

        def each_block_count(gradient_pairs, blocks_now):
            query_here, grad_here, pos_here, doc_here, begin_here = blocks_now
            query_gradient, pair_grads = attention_grads(query_here, grad_here, key_value_rows, pos_here, doc_here, begin_here, token_positions, document_labels)
            return (gradient_pairs + pair_grads, query_gradient)
        gradient_pairs, query_gradient = lax.scan(each_block_count, jnp.zeros((SEQUENCE_TOKENS, 2, KEY_VALUE_HEADS, HEAD_CHANNELS), jnp.float32), (query_block_list, gradient_blocks, token_positions.reshape(total_blocks, KEYS_PER_BLOCK), document_labels.reshape(total_blocks, KEYS_PER_BLOCK), start_offsets.reshape(total_blocks, KEYS_PER_BLOCK)))
        query_list.append(query_gradient.reshape(SEQUENCE_TOKENS, QUERY_HEADS * HEAD_CHANNELS).astype(jnp.bfloat16))
        key_collection.append(gradient_pairs[:, 0].reshape(SEQUENCE_TOKENS, KEY_VALUE_HEADS * HEAD_CHANNELS).astype(jnp.bfloat16))
        value_collection.append(gradient_pairs[:, 1].reshape(SEQUENCE_TOKENS, KEY_VALUE_HEADS * HEAD_CHANNELS).astype(jnp.bfloat16))
    return (grads[0].astype(jnp.bfloat16), grads[1].astype(jnp.bfloat16), grads[2], grads[3].astype(jnp.bfloat16), grads[4].astype(jnp.bfloat16), grads[5], grads[7], grads[8], jnp.stack(query_list), jnp.stack(key_collection), jnp.stack(value_collection))
```

```python
import math

import jax
import jax.numpy as jnp
from jax import lax
from jax.sharding import PartitionSpec as P

HS = 128
P_SIZE = 64
NST = 128
CH = 128
HEAD_CHANNELS = 128
KEYS_PER_BLOCK = 512
REACH = 4


precise = lax.Precision.HIGHEST
masked_score = -1e30
norm_epsilon = 1e-05


def carried_chain(decay, state, axis, reverse):
    by = -1 if reverse else 1
    current = state
    for hop in range(REACH):
        received = passed_along(current.astype(jnp.bfloat16), axis, by).astype(jnp.float32)
        if hop < REACH - 1:
            current = state + decay[:, None, None] * received
    return received


def butterfly_sum(shard, axis):
    count = lax.axis_size(axis)
    span = 1
    while span < count:
        pairs = [(i, i ^ span) for i in range(count)]
        shard = shard + lax.ppermute(shard, axis, pairs)
        span *= 2
    return shard


def passed_along(shard, axis, by):
    devices = lax.axis_size(axis)
    pairs = [(i, i + by) for i in range(devices) if 0 <= i + by < devices]
    return lax.ppermute(shard, axis, pairs)


def doc_index(token_positions, doc_ends):
    return jnp.sum((token_positions[:, None] >= doc_ends[None, :]).astype(jnp.int32), axis=1)


def doc_begin(token_positions, doc_ends, lengths):
    return jnp.sum(
        jnp.where(token_positions[:, None] >= doc_ends[None, :], lengths[None, :], 0), axis=1
    )


def state_scan(
    inputs, step_sizes, b_rows, c_rows, decay_rates, skip_gains, document_labels, before, block_len
):
    rows_count, head_count, head_width = inputs.shape
    group_count, state_width = (b_rows.shape[1], b_rows.shape[2])
    group_heads = head_count // group_count
    block_count = rows_count // block_len
    x_blocks = inputs.reshape(block_count, block_len, group_count, group_heads, head_width)
    step_blocks = step_sizes.reshape(head_count, block_count, block_len).transpose(1, 0, 2)
    b_blocks = b_rows.reshape(block_count, block_len, group_count, state_width)
    c_blocks = c_rows.reshape(block_count, block_len, group_count, state_width)
    doc_blocks = document_labels.reshape(block_count, block_len)
    offsets = jnp.arange(block_len)
    causal = offsets[:, None] >= offsets[None, :]

    def advance(carried_in, inputs_now):
        state_now, last_doc = carried_in
        x_here, step_here, b_here, c_here, doc_here = inputs_now
        cumulative = jnp.cumsum(-decay_rates[:, None] * step_here, axis=1)
        within = (doc_here[:, None] == doc_here[None, :]) & causal
        exponent = jnp.where(
            within[None], cumulative[:, :, None] - cumulative[:, None, :], masked_score
        )
        decays = jnp.exp(exponent).reshape(group_count, group_heads, block_len, block_len)
        intersection = jnp.einsum("tgn,sgn->gts", c_here, b_here, precision=precise)
        weights = (
            decays
            * intersection[:, None]
            * step_here.reshape(group_count, group_heads, 1, block_len)
        )
        inside = jnp.einsum("gjts,sgjp->tgjp", weights, x_here, precision=precise)
        survive = jnp.where((doc_here == last_doc)[None, :], jnp.exp(cumulative), 0.0)
        survive = survive.reshape(group_count, group_heads, block_len).transpose(2, 0, 1)
        carried = (
            jnp.einsum("gjpn,tgn->tgjp", state_now, c_here, precision=precise) * survive[..., None]
        )
        outputs = (
            inside
            + carried
            + skip_gains.reshape(group_count, group_heads)[None, :, :, None] * x_here
        )
        tail_weight = (
            jnp.where(
                (doc_here == doc_here[-1])[None, :], jnp.exp(cumulative[:, -1:] - cumulative), 0.0
            )
            * step_here
        )
        injected = jnp.einsum(
            "gjs,sgjp,sgn->gjpn",
            tail_weight.reshape(group_count, group_heads, block_len),
            x_here,
            b_here,
            precision=precise,
        )
        retained = jnp.where(doc_here[-1] == last_doc, jnp.exp(cumulative[:, -1]), 0.0).reshape(
            group_count, group_heads
        )
        return ((injected + retained[:, :, None, None] * state_now, doc_here[-1]), outputs)

    initial = (jnp.zeros((group_count, group_heads, head_width, state_width), jnp.float32), before)
    (final_state, _), outputs = lax.scan(
        advance, initial, (x_blocks, step_blocks, b_blocks, c_blocks, doc_blocks)
    )
    return (
        outputs.reshape(rows_count, head_count, head_width),
        final_state.reshape(head_count, head_width, state_width),
    )


def attention_grads(
    query_row_block,
    grad_rows,
    key_value_rows,
    query_pos,
    query_docs,
    query_begin,
    key_pos,
    key_docs,
):
    scale_factor = 1.0 / math.sqrt(HEAD_CHANNELS)
    key_count = key_value_rows.shape[0]
    kv_heads = key_value_rows.shape[2]
    heads_per_group = query_row_block.shape[2]
    rows_count = query_row_block.shape[0]
    block_count = key_count // KEYS_PER_BLOCK
    kv_blocks = key_value_rows.reshape(block_count, KEYS_PER_BLOCK, 2, kv_heads, HEAD_CHANNELS)
    pos_blocks = key_pos.reshape(block_count, KEYS_PER_BLOCK)
    doc_blocks = key_docs.reshape(block_count, KEYS_PER_BLOCK)
    lowest = jnp.min(query_begin)
    highest = jnp.max(query_pos)

    def allowed_of(block_pos, block_docs):
        allowed = (
            (block_pos[None, :] <= query_pos[:, None])
            & (block_docs[None, :] == query_docs[:, None])
            & (block_pos[None, :] >= 0)
        )
        return allowed[None, None]

    def active(block_pos):
        return (block_pos[-1] >= lowest) & (block_pos[0] <= highest)

    def scores_of(block_keys, allowed):
        raw_scores = (
            jnp.einsum(
                "icge,jce->cgij", query_row_block, block_keys, preferred_element_type=jnp.float32
            )
            * scale_factor
        )
        return jnp.where(allowed, raw_scores, masked_score)

    def first_pass(running, blocks_now):
        block_kv, block_pos, block_docs = blocks_now

        def first_accumulate(running):
            top_score, total, weighted = running
            allowed = allowed_of(block_pos, block_docs)
            scores = scores_of(block_kv[:, 0], allowed)
            new_top = jnp.maximum(top_score, jnp.max(scores, axis=-1))
            expo = jnp.where(allowed, jnp.exp(scores - new_top[..., None]), 0.0)
            grad_dots = jnp.einsum(
                "icge,jce->cgij", grad_rows, block_kv[:, 1], preferred_element_type=jnp.float32
            )
            fade = jnp.exp(top_score - new_top)
            return (
                new_top,
                total * fade + jnp.sum(expo, axis=-1),
                weighted * fade + jnp.sum(expo * grad_dots, axis=-1),
            )

        def unchanged(running):
            return running

        return (lax.cond(active(block_pos), first_accumulate, unchanged, running), None)

    stat_shape = (kv_heads, heads_per_group, rows_count)
    initial = (
        jnp.full(stat_shape, masked_score, jnp.float32),
        jnp.zeros(stat_shape, jnp.float32),
        jnp.zeros(stat_shape, jnp.float32),
    )
    (top_score, total, weighted), _ = lax.scan(
        first_pass, initial, (kv_blocks, pos_blocks, doc_blocks)
    )
    log_total = top_score + jnp.log(total)
    centre = weighted / total

    def second_pass(query_gradient, blocks_now):
        block_kv, block_pos, block_docs = blocks_now

        def second_accumulate(query_gradient):
            allowed = allowed_of(block_pos, block_docs)
            scores = scores_of(block_kv[:, 0], allowed)
            probs = jnp.where(allowed, jnp.exp(scores - log_total[..., None]), 0.0)
            grad_dots = jnp.einsum(
                "icge,jce->cgij", grad_rows, block_kv[:, 1], preferred_element_type=jnp.float32
            )
            prob_low = probs.astype(jnp.bfloat16)
            score_grad = (probs * (grad_dots - centre[..., None])).astype(jnp.bfloat16)
            grad_key = (
                jnp.einsum(
                    "cgij,icge->jce",
                    score_grad,
                    query_row_block,
                    preferred_element_type=jnp.float32,
                )
                * scale_factor
            )
            grad_value = jnp.einsum(
                "cgij,icge->jce", prob_low, grad_rows, preferred_element_type=jnp.float32
            )
            query_gradient = query_gradient + jnp.einsum(
                "cgij,jce->icge", score_grad, block_kv[:, 0], preferred_element_type=jnp.float32
            )
            return (query_gradient, jnp.stack([grad_key, grad_value], axis=1))

        def skipped(query_gradient):
            return (
                query_gradient,
                jnp.zeros((KEYS_PER_BLOCK, 2, kv_heads, HEAD_CHANNELS), jnp.float32),
            )

        return lax.cond(active(block_pos), second_accumulate, skipped, query_gradient)

    query_gradient, gradient_blocks = lax.scan(
        second_pass,
        jnp.zeros((rows_count, kv_heads, heads_per_group, HEAD_CHANNELS), jnp.float32),
        (kv_blocks, pos_blocks, doc_blocks),
    )
    return (
        query_gradient * scale_factor,
        gradient_blocks.reshape(key_count, 2, kv_heads, HEAD_CHANNELS),
    )


def per_device(
    ssm_input,
    ssm_gate,
    step_raw,
    b_proj,
    c_proj,
    rate_log,
    step_bias,
    skip_gain,
    norm_gain,
    ssm_grad_out,
    queries,
    keys,
    values,
    attention_output_gradient,
    doc_lengths,
):
    tokens_here = ssm_input.shape[1]
    device_index = lax.axis_index("ctx")
    lengths = doc_lengths[0]
    doc_ends = jnp.cumsum(lengths)
    token_positions = device_index * tokens_here + jnp.arange(tokens_here, dtype=jnp.int32)
    document_labels = doc_index(token_positions, doc_ends)
    before = doc_index(token_positions[:1] - 1, doc_ends)[0]
    head_count = rate_log.shape[0]
    inputs = ssm_input[0].astype(jnp.float32).reshape(tokens_here, head_count, P_SIZE)
    b_rows = b_proj[0].astype(jnp.float32).reshape(tokens_here, -1, NST)
    c_rows = c_proj[0].astype(jnp.float32).reshape(tokens_here, -1, NST)
    raw_steps = step_raw[0]

    def local_part(inputs, raw_steps, b_rows, c_rows, rate_log, step_bias, skip_gain):
        step_sizes = jax.nn.softplus(raw_steps + step_bias[:, None])
        decay_rates = jnp.exp(rate_log)
        mixed_zero, local_state = state_scan(
            inputs, step_sizes, b_rows, c_rows, decay_rates, skip_gain, document_labels, before, CH
        )
        decay_total = jnp.where(
            document_labels[-1] == before, jnp.exp(-decay_rates * jnp.sum(step_sizes, axis=1)), 0.0
        )
        return (mixed_zero, local_state, decay_total)

    def entry_part(raw_steps, c_rows, rate_log, step_bias, entry_state):
        step_sizes = jax.nn.softplus(raw_steps + step_bias[:, None])
        decay_rates = jnp.exp(rate_log)
        cumulative = jnp.cumsum(-decay_rates[:, None] * step_sizes, axis=1)
        survive = jnp.where((document_labels == before)[None, :], jnp.exp(cumulative), 0.0)
        group_count = c_rows.shape[1]
        group_heads = head_count // group_count
        survive = survive.reshape(group_count, group_heads, tokens_here).transpose(2, 0, 1)
        carried = (
            jnp.einsum(
                "gjpn,tgn->tgjp",
                entry_state.reshape(group_count, group_heads, P_SIZE, NST),
                c_rows,
                precision=precise,
            )
            * survive[..., None]
        )
        return carried.reshape(tokens_here, head_count, P_SIZE)

    (mixed_zero, local_state, decay_total), pull_local = jax.vjp(
        local_part, inputs, raw_steps, b_rows, c_rows, rate_log, step_bias, skip_gain
    )
    entry_state = carried_chain(decay_total, local_state, "ctx", False)
    mixed_entry, pull_entry = jax.vjp(
        entry_part, raw_steps, c_rows, rate_log, step_bias, entry_state
    )
    mixed = (mixed_zero + mixed_entry).reshape(tokens_here, head_count * P_SIZE)
    gate_values = ssm_gate[0].astype(jnp.float32)
    sigma = jax.nn.sigmoid(gate_values)
    activation = gate_values * sigma
    gated = mixed * activation
    out_grad = ssm_grad_out[0].astype(jnp.float32)
    scaled_grad = out_grad * norm_gain[None, :]
    square_sum, cross_sum = lax.psum(
        (jnp.sum(gated * gated, axis=1), jnp.sum(gated * scaled_grad, axis=1)), "tp"
    )
    full_width = HS * P_SIZE
    factor = lax.rsqrt(square_sum / full_width + norm_epsilon)
    gated_grad = (
        factor[:, None] * scaled_grad
        - gated * (factor * factor * factor * cross_sum / full_width)[:, None]
    )
    gain_grad = jnp.sum(out_grad * gated * factor[:, None], axis=0)
    gate_grad = gated_grad * mixed * sigma * (1.0 + gate_values * (1.0 - sigma))
    mixed_grad = (gated_grad * activation).reshape(tokens_here, head_count, P_SIZE)
    entry_grads = pull_entry(mixed_grad)
    next_grad = carried_chain(decay_total, entry_grads[4], "ctx", True)
    decay_grad = jnp.sum(next_grad * entry_state, axis=(1, 2))
    local_grads = pull_local((mixed_grad, next_grad, decay_grad))
    rate_grad = local_grads[4] + entry_grads[2]
    packed = jnp.concatenate([rate_grad, local_grads[6], gain_grad])
    packed = butterfly_sum(butterfly_sum(packed, "dp"), "ctx")
    rate_sum, skip_sum, gain_sum = (
        packed[:head_count],
        packed[head_count : 2 * head_count],
        packed[2 * head_count :],
    )
    grad_input = local_grads[0].reshape(tokens_here, head_count * P_SIZE)[None].astype(jnp.bfloat16)
    grad_gate = gate_grad[None].astype(jnp.bfloat16)
    grad_raw = (local_grads[1] + entry_grads[0])[None]
    grad_b = local_grads[2].reshape(tokens_here, -1)[None].astype(jnp.bfloat16)
    grad_c = (local_grads[3] + entry_grads[1]).reshape(tokens_here, -1)[None].astype(jnp.bfloat16)
    kv_heads = keys.shape[2] // HEAD_CHANNELS
    query_row_block = queries[0].reshape(tokens_here, kv_heads, -1, HEAD_CHANNELS)
    grad_rows = attention_output_gradient[0].reshape(tokens_here, kv_heads, -1, HEAD_CHANNELS)
    query_begin = doc_begin(token_positions, doc_ends, lengths)
    pair_local = jnp.concatenate([keys[0], values[0]], axis=1)
    reach = min(4, lax.axis_size("ctx") // 2)
    slots = 2 * reach
    pieces = [pair_local]
    carry_piece = pair_local
    for hop_index in range(reach):
        carry_piece = passed_along(carry_piece, "ctx", 1)
        pieces.insert(0, carry_piece)
    padding = jnp.zeros(((slots - reach - 1) * tokens_here, pair_local.shape[1]), pair_local.dtype)
    window = jnp.concatenate([padding] + pieces, axis=0)
    first_key = (device_index + 1 - slots) * tokens_here
    key_count = window.shape[0]
    key_pos = first_key + jnp.arange(key_count, dtype=jnp.int32)
    key_docs = doc_index(key_pos, doc_ends)
    query_gradient, gradient_pairs = attention_grads(
        query_row_block,
        grad_rows,
        window.reshape(key_count, 2, kv_heads, HEAD_CHANNELS),
        token_positions,
        document_labels,
        query_begin,
        key_pos,
        key_docs,
    )
    gradient_pairs = gradient_pairs.reshape(key_count, 2 * kv_heads * HEAD_CHANNELS)
    slot_rows = gradient_pairs.reshape(slots, tokens_here, -1)
    running_sum = slot_rows[slots - 1 - reach]
    for hop_index in range(reach):
        running_sum = (
            passed_along(running_sum.astype(jnp.bfloat16), "ctx", -1).astype(running_sum.dtype)
            + slot_rows[slots - reach + hop_index]
        )
    grad_queries = query_gradient.reshape(tokens_here, -1)[None].astype(jnp.bfloat16)
    grad_keys = running_sum[:, : kv_heads * HEAD_CHANNELS][None].astype(jnp.bfloat16)
    grad_values = running_sum[:, kv_heads * HEAD_CHANNELS :][None].astype(jnp.bfloat16)
    return (
        grad_input,
        grad_gate,
        grad_raw,
        grad_b,
        grad_c,
        rate_sum,
        skip_sum,
        gain_sum,
        grad_queries,
        grad_keys,
        grad_values,
    )


def solution(mesh):
    placed = (
        P("dp", "ctx", "tp"),
        P("dp", "ctx", "tp"),
        P("dp", "tp", "ctx"),
        P("dp", "ctx", "tp"),
        P("dp", "ctx", "tp"),
        P("tp"),
        P("tp"),
        P("tp"),
        P("tp"),
        P("dp", "ctx", "tp"),
        P("dp", "ctx", "tp"),
        P("dp", "ctx", "tp"),
        P("dp", "ctx", "tp"),
        P("dp", "ctx", "tp"),
        P("dp", None),
    )
    return jax.shard_map(
        per_device,
        mesh=mesh,
        in_specs=placed,
        out_specs=(
            P("dp", "ctx", "tp"),
            P("dp", "ctx", "tp"),
            P("dp", "tp", "ctx"),
            P("dp", "ctx", "tp"),
            P("dp", "ctx", "tp"),
            P("tp"),
            P("tp"),
            P("tp"),
            P("dp", "ctx", "tp"),
            P("dp", "ctx", "tp"),
            P("dp", "ctx", "tp"),
        ),
        check_vma=False,
    )
```

```python
import jax
import jax.numpy as jnp
from jax import lax
from jax.experimental import pallas as pl
from jax.experimental.pallas import tpu as pltpu
from jax.sharding import PartitionSpec as P

MESH = pl.DeviceIdType.MESH
F32 = jnp.float32
BF16 = jnp.bfloat16
HIGH = lax.Precision.HIGHEST

TOKENS = 128
WIDE = 64
REACH = 4
CHUNK = 256
KV = 2
NORM_WIDTH = 8192
EPSILON = 1e-05
MASKED = -1e30
SCALE = 128.0**-0.5
Z_SIZE = 8
X_SIZE = 4
CORES = 2
TP_SIZE = 4


def dot(a, b, dims, precision=None):
    return lax.dot_general(
        a, b, (dims, ((), ())), precision=precision, preferred_element_type=F32
    )


def nn(a, b, precision=None):
    return dot(a, b, ((1,), (0,)), precision)


def nt(a, b, precision=None):
    return dot(a, b, ((1,), (1,)), precision)


def tn(a, b, precision=None):
    return dot(a, b, ((0,), (0,)), precision)


def iota(shape, axis):
    return lax.broadcasted_iota(jnp.int32, shape, axis)


def lanes(start, size):
    return pl.ds(pl.multiple_of(start, size), size)


def column(row):
    size = row.shape[1]
    on_diagonal = iota((size, size), 0) == iota((size, size), 1)
    return jnp.sum(jnp.where(on_diagonal, row, 0.0), axis=1, keepdims=True)


def turned(row):
    return jnp.transpose(jnp.broadcast_to(row, (TOKENS, TOKENS)))


def twice(a):
    return jnp.concatenate([a, a], axis=1)


def folded(a):
    return a[:, :TOKENS] + a[:, TOKENS:]


def kernel(
    lens, x, gate, raw, b, c, rate_log, bias, skip, gain, dout, q, k, v, do,
    gx, ggate, graw, gb, gc, grate, gskip, ggain, gq, gk, gv,
    ls, w, mixed, carried, dy, dxin, sve, tse, rows, marks, heads,
    gram, dgram, loc, dsl, fsend, frecv, bsend, brecv, kw, vw, kall, vall,
    dacc, dsend, drecv, tsum, tmsg, tbuf, cols, dc, db, hsum, zmsg, zbuf, xmsg, xbuf,
    fss, frs, bss, brs, kss, krs, dss, drs, tss, trs, zss, zrs, xss, xrs,
):
    i = lax.axis_index("ctx")
    core = lax.axis_index("dp")
    tp = lax.axis_index("tp")
    count = Z_SIZE * X_SIZE
    right = lax.rem(i + 1, count)
    left = lax.rem(i + count - 1, count)
    z = lax.rem(i, Z_SIZE)
    xi = i // Z_SIZE
    xc = xi * CORES + core
    z_peers = [xi * Z_SIZE + lax.rem(z + n, Z_SIZE) for n in range(1, Z_SIZE)]
    xc_peers = [lax.rem(xc + n, X_SIZE * CORES) for n in range(1, X_SIZE * CORES)]
    xc_ids = [{"ctx": (p // CORES) * Z_SIZE + z, "dp": lax.rem(p, CORES)} for p in xc_peers]
    tp_peers = [lax.rem(tp + n, TP_SIZE) for n in range(1, TP_SIZE)]
    n_heads = raw.shape[0]
    channels = x.shape[1]
    groups = b.shape[1] // TOKENS
    pairs = n_heads // 2 // groups

    barrier = pltpu.get_barrier_semaphore()
    greeted = (
        [{"ctx": left}, {"ctx": right}]
        + [{"tp": p} for p in tp_peers]
        + [{"ctx": p} for p in z_peers]
        + xc_ids
    )
    for device in greeted:
        pl.semaphore_signal(barrier, inc=1, device_id=device, device_id_type=MESH)
    pl.semaphore_wait(barrier, len(greeted))

    def remote(source, target, send, recv, device):
        return pltpu.make_async_remote_copy(
            src_ref=source,
            dst_ref=target,
            send_sem=send,
            recv_sem=recv,
            device_id=device,
            device_id_type=MESH,
        )

    def kv_copies(hop):
        slot = REACH - 1 - hop
        k_from = k if hop == 0 else kw.at[slot + 1]
        v_from = v if hop == 0 else vw.at[slot + 1]
        to = {"ctx": right}
        return (
            remote(k_from, kw.at[slot], kss.at[0, hop], krs.at[0, hop], to),
            remote(v_from, vw.at[slot], kss.at[1, hop], krs.at[1, hop], to),
        )

    def kv_start(hop):
        for copy in kv_copies(hop):
            copy.start()

    def kv_wait(hop):
        for copy in kv_copies(hop):
            copy.wait_recv()

    kv_start(0)

    base = i * TOKENS
    position = iota((8, TOKENS), 1) + base
    begin = jnp.zeros((8, TOKENS), jnp.int32)
    end = jnp.int32(0)
    for d in range(lens.shape[1]):
        end = end + lens[0, d]
        begin = begin + jnp.where(position >= end, lens[0, d], 0)
    begin_row = (begin - base)[0:1]
    begin_last = begin_row[:, TOKENS - 1 :]
    begin_col = turned(begin_row.astype(F32))
    row_id = iota((TOKENS, TOKENS), 0)
    lane_id = iota((TOKENS, TOKENS), 1)
    within = (lane_id <= row_id) & (lane_id.astype(F32) >= begin_col)
    up_to = (row_id <= lane_id).astype(F32)

    shifted = raw[...] + column(bias[...])
    step = jax.nn.softplus(shifted)
    rate = jnp.exp(column(rate_log[...]))
    decay = -rate * step
    cum = nn(decay, up_to, HIGH)
    cum_end = cum[:, TOKENS - 1 :]
    survive = jnp.where(begin_row < 0, jnp.exp(cum), 0.0)
    tail = jnp.where(iota((1, TOKENS), 1) >= begin_last, jnp.exp(cum_end - cum), 0.0)
    whole = jnp.where(begin_last < 0, jnp.exp(cum_end), 0.0)
    heads[0] = step
    heads[1] = cum
    heads[2] = tail
    mark = iota((n_heads, channels), 1) // WIDE == iota((n_heads, channels), 0)
    marks[...] = mark.astype(BF16)
    both = jnp.concatenate([marks[...], marks[...]], axis=0)

    def expand(a):
        high = a.astype(BF16)
        low = (a - high.astype(F32)).astype(BF16)
        return tn(jnp.concatenate([high, low], axis=0), both)

    tse[...] = expand(tail * step)
    rows[0:1] = jnp.sum(jnp.where(mark, whole, 0.0), axis=0, keepdims=True)

    def group(a, g):
        return a[:, g * TOKENS : (g + 1) * TOKENS]

    def local_state(ch, g):
        part = lanes(ch * CHUNK, CHUNK)
        inputs = (x[:, part].astype(F32) * tse[:, part]).astype(BF16)
        loc[ch] = tn(group(b, g), inputs)

    def f_chunk(stage, g):
        return g * 4 + lax.rem(stage + 4 * count - i, 4)

    def b_chunk(stage, g):
        return g * 4 + lax.rem(stage + i, 4)

    def chain(send, recv, ss, rs, device):
        def copy(leg, ch, to):
            return remote(send.at[leg, ch], recv.at[to, ch], ss.at[leg, ch], rs.at[to, ch], device)

        return copy

    f_copy = chain(fsend, frecv, fss, frs, {"ctx": right})
    b_copy = chain(bsend, brecv, bss, brs, {"ctx": left})

    def leg_a(copy, send, recv, own, ch, stage):
        value = own[ch]
        if stage > 0:
            copy(0, ch, 0).wait_recv()
            value = value + rows[0:1, lanes(ch * CHUNK, CHUNK)] * recv[0, ch].astype(F32)
        send[0, ch] = value.astype(BF16)
        copy(0, ch, 1 if stage == 3 else 0).start()

    def leg_b(copy, send, recv, own, ch, stage):
        copy(1, ch, 1).wait_recv()
        if stage < 3:
            value = own[ch] + rows[0:1, lanes(ch * CHUNK, CHUNK)] * recv[1, ch].astype(F32)
            send[1, ch] = value.astype(BF16)
            copy(1, ch, 1).start()

    def f_leg_a(stage):
        for g in range(groups):
            leg_a(f_copy, fsend, frecv, loc, f_chunk(stage, g), stage)

    def b_leg_a(stage):
        for g in range(groups):
            leg_a(b_copy, bsend, brecv, dsl, b_chunk(stage, g), stage)

    for g in range(groups):
        local_state(f_chunk(0, g), g)
    f_leg_a(0)
    for stage in range(1, 4):
        for g in range(groups):
            local_state(f_chunk(stage, g), g)
    sve[...] = expand(survive)
    rows[1:2] = jnp.sum(jnp.where(mark, column(skip[...]), 0.0), axis=0, keepdims=True)
    for g in range(groups):
        gram[g] = nt(group(c, g), group(b, g))

    left_half = iota((1, TOKENS), 1) < WIDE

    def inside_pair(g):
        def body(n, _):
            pair = g * pairs + n
            part = lanes(pair * TOKENS, TOKENS)
            for e in range(2):
                h = pair * 2 + e
                cum_row = heads[1, pl.ds(h, 1), :]
                gap = jnp.where(within, turned(cum_row) - cum_row, MASKED)
                scaled = jnp.exp(gap) * heads[0, pl.ds(h, 1), :]
                ls[h] = scaled.astype(BF16)
                w[h] = (scaled * gram[g]).astype(BF16)
            x_part = x[:, part]
            product = nn(w[pl.ds(pair * 2, 2)].reshape(2 * TOKENS, TOKENS), x_part)
            inside = jnp.where(left_half, product[:TOKENS], product[TOKENS:])
            mixed[:, part] = inside + rows[1:2, part] * x_part.astype(F32)
            return 0

        lax.fori_loop(0, pairs, body, 0)

    def attention(kv, first, last):
        key = kall[kv]
        value = vall[kv]
        window = (REACH + 1) * TOKENS
        key_at = iota((window, 2 * TOKENS), 0) - REACH * TOKENS
        query_at = twice(iota((1, TOKENS), 1))
        allowed = (key_at <= query_at) & (key_at >= twice(begin_row))

        def body(n, _):
            offset = (kv * 4 + n) * 2 * TOKENS
            part = lanes(offset, 2 * TOKENS)
            q_two = q[:, part]
            do_two = do[:, part]
            query = jnp.concatenate([q_two[:, :TOKENS], q_two[:, TOKENS:]], axis=0)
            cotangent = jnp.concatenate([do_two[:, :TOKENS], do_two[:, TOKENS:]], axis=0)
            score = jnp.where(allowed, nt(key, query) * SCALE, MASKED)
            top = jnp.max(score, axis=0, keepdims=True)
            weight = jnp.exp(score - top)
            total = jnp.sum(weight, axis=0, keepdims=True)
            prob = weight * (1.0 / total)
            reply = nt(value, cotangent)
            centre = jnp.sum(prob * reply, axis=0, keepdims=True)
            score_grad = (prob * (reply - centre)).astype(BF16)
            query_grad = (tn(score_grad, key) * SCALE).astype(BF16)
            gq[:, part] = jnp.concatenate([query_grad[:TOKENS], query_grad[TOKENS:]], axis=1)
            dacc[kv, :, 0:TOKENS] += nn(score_grad, query) * SCALE
            dacc[kv, :, TOKENS : 2 * TOKENS] += nn(prob.astype(BF16), cotangent)
            return 0

        lax.fori_loop(first, last, body, 0)

    def d_copy(kv, hop):
        return remote(
            dsend.at[kv, hop], drecv.at[kv, hop], dss.at[kv, hop], drs.at[kv, hop], {"ctx": left}
        )

    def d_hop(kv, hop):
        own = dacc[kv, hop * TOKENS : (hop + 1) * TOKENS]
        if hop > 0:
            d_copy(kv, hop - 1).wait_recv()
            own = own + drecv[kv, hop - 1].astype(F32)
        if hop < REACH:
            dsend[kv, hop] = own.astype(BF16)
            d_copy(kv, hop).start()
        else:
            gk[:, kv * TOKENS : (kv + 1) * TOKENS] = own[:, :TOKENS].astype(BF16)
            gv[:, kv * TOKENS : (kv + 1) * TOKENS] = own[:, TOKENS:].astype(BF16)

    def gating(part):
        g_here = gate[:, part].astype(F32)
        sigma = jax.nn.sigmoid(g_here)
        activation = g_here * sigma
        out_grad = dout[:, part].astype(F32)
        return g_here, sigma, activation, out_grad, out_grad * gain[0:1, part]

    def middle(ch, g):
        part = lanes(ch * CHUNK, CHUNK)
        entered = nn(group(c, g), frecv[1, ch]) * sve[:, part]
        carried[:, part] = entered.astype(BF16)
        here = mixed[:, part] + entered
        mixed[:, part] = here
        _, _, activation, _, scaled = gating(part)
        gated = here * activation
        tsum[0] += folded(gated * gated)
        tsum[1] += folded(gated * scaled)

    def f_leg_b(stage):
        for g in range(groups):
            leg_b(f_copy, fsend, frecv, loc, f_chunk(stage, g), stage)
        for g in range(groups):
            middle(f_chunk(stage, g), g)

    tsum[...] = jnp.zeros_like(tsum)
    dacc[...] = jnp.zeros_like(dacc)
    dgram[...] = jnp.zeros_like(dgram)
    dc[...] = jnp.zeros_like(dc)
    db[...] = jnp.zeros_like(db)
    hsum[...] = jnp.zeros_like(hsum)

    kv_wait(0)
    kv_start(1)
    f_leg_a(1)
    inside_pair(0)
    kv_wait(1)
    kv_start(2)
    f_leg_a(2)
    inside_pair(1)
    kv_wait(2)
    kv_start(3)
    f_leg_a(3)
    f_leg_b(0)
    kv_wait(3)
    for kv in range(KV):
        head = slice(kv * TOKENS, (kv + 1) * TOKENS)
        for slot in range(REACH + 1):
            window = slice(slot * TOKENS, (slot + 1) * TOKENS)
            kall[kv, window] = kw[slot, :, head] if slot < REACH else k[:, head]
            vall[kv, window] = vw[slot, :, head] if slot < REACH else v[:, head]
    attention(0, 0, 2)
    f_leg_b(1)
    attention(0, 2, 4)
    f_leg_b(2)
    d_hop(0, 0)
    attention(1, 0, 2)
    f_leg_b(3)

    ones = jnp.ones((8, TOKENS), F32)
    squares = nt(ones, tsum[0], HIGH)
    crosses = nt(ones, tsum[1], HIGH)
    message = jnp.where(iota((8, TOKENS), 0) == 0, squares, crosses)
    tmsg[...] = message
    tbuf[tp] = message

    def t_copy(peer, slot):
        return remote(tmsg, tbuf.at[slot], tss.at[peer], trs.at[slot], {"tp": peer})

    for peer in tp_peers:
        t_copy(peer, tp).start()
    attention(1, 2, 4)
    d_hop(1, 0)
    d_hop(0, 1)
    for peer in tp_peers:
        t_copy(peer, peer).wait_recv()
    total = tbuf[0] + tbuf[1] + tbuf[2] + tbuf[3]
    factor = lax.rsqrt(total[0:1] / NORM_WIDTH + EPSILON)
    pull = factor * factor * factor * total[1:2] / NORM_WIDTH
    cols[0] = turned(factor)
    cols[1] = turned(pull)

    def cotangents(ch, g):
        part = lanes(ch * CHUNK, CHUNK)
        g_here, sigma, activation, out_grad, scaled = gating(part)
        here = mixed[:, part]
        gated = here * activation
        factor_col = twice(cols[0])
        gated_grad = factor_col * scaled - gated * twice(cols[1])
        mixed_grad = gated_grad * activation
        dy[:, part] = mixed_grad.astype(BF16)
        dsl[ch] = tn(group(c, g), (mixed_grad * sve[:, part]).astype(BF16))
        gate_grad = gated_grad * here * sigma * (1.0 + g_here * (1.0 - sigma))
        ggate[:, part] = gate_grad.astype(BF16)
        rows[2:3, part] = jnp.sum(out_grad * gated * factor_col, axis=0, keepdims=True)

    def side_sums(ch, g):
        part = lanes(ch * CHUNK, CHUNK)
        mixed_grad = dy[:, part].astype(F32)
        mark_part = marks[:, part]
        dc[g] += nt((mixed_grad * sve[:, part]).astype(BF16), frecv[1, ch])
        hsum[0] += nt(mark_part, (mixed_grad * carried[:, part].astype(F32)).astype(BF16))
        hsum[1] += nt(mark_part, (mixed_grad * x[:, part].astype(F32)).astype(BF16))

    for g in range(groups):
        cotangents(b_chunk(0, g), g)
    b_leg_a(0)
    for stage in range(1, 4):
        for g in range(groups):
            cotangents(b_chunk(stage, g), g)

    before = (row_id < lane_id).astype(BF16)
    not_before = row_id >= lane_id

    def inside_back(g, first, last):
        def body(n, _):
            pair = g * pairs + n
            part = lanes(pair * TOKENS, TOKENS)
            dy_part = dy[:, part]
            zero = jnp.zeros_like(dy_part)
            split = jnp.concatenate(
                [jnp.where(left_half, dy_part, zero), jnp.where(left_half, zero, dy_part)], axis=0
            )
            weight_grad = nt(split, x[:, part])
            w_two = w[pl.ds(pair * 2, 2)].reshape(2 * TOKENS, TOKENS)
            ls_two = ls[pl.ds(pair * 2, 2)].reshape(2 * TOKENS, TOKENS)
            spread = weight_grad * ls_two.astype(F32)
            dgram[g] += spread[:TOKENS] + spread[TOKENS:]
            moment = weight_grad * w_two.astype(F32)
            crossing = nn(moment.astype(BF16), before)
            for e in range(2):
                half = slice(e * TOKENS, (e + 1) * TOKENS)
                row = pl.ds(pair * 2 + e, 1)
                heads[3, row, :] = jnp.sum(moment[half], axis=0, keepdims=True)
                heads[4, row, :] = jnp.sum(
                    jnp.where(not_before, crossing[half], 0.0), axis=0, keepdims=True
                )
            dxin[:, part] = tn(w_two, split)
            return 0

        lax.fori_loop(first, last, body, 0)

    def finish(ch, g):
        part = lanes(ch * CHUNK, CHUNK)
        later = brecv[1, ch]
        mark_part = marks[:, part]
        x_part = x[:, part].astype(F32)
        tail_part = tse[:, part]
        scaled_grad = nn(group(b, g), later)
        input_grad = (
            dxin[:, part] + rows[1:2, part] * dy[:, part].astype(F32) + scaled_grad * tail_part
        )
        gx[:, part] = input_grad.astype(BF16)
        hsum[2] += nt(mark_part, (x_part * scaled_grad).astype(BF16))
        hsum[3] += nt(mark_part, (later.astype(F32) * frecv[1, ch].astype(F32)).astype(BF16))
        db[g] += nt((x_part * tail_part).astype(BF16), later)

    def b_leg_b(stage):
        for g in range(groups):
            leg_b(b_copy, bsend, brecv, dsl, b_chunk(stage, g), stage)
        for g in range(groups):
            finish(b_chunk(stage, g), g)

    d_hop(1, 1)
    b_leg_a(1)
    inside_back(0, 0, pairs)
    d_hop(0, 2)
    d_hop(1, 2)
    b_leg_a(2)
    inside_back(1, 0, pairs)
    d_hop(0, 3)
    d_hop(1, 3)
    b_leg_a(3)
    for stage in range(2):
        for g in range(groups):
            side_sums(b_chunk(stage, g), g)
    b_leg_b(0)
    for stage in range(2, 4):
        for g in range(groups):
            side_sums(b_chunk(stage, g), g)
    d_hop(0, 4)
    d_hop(1, 4)
    b_leg_b(1)
    b_leg_b(2)
    b_leg_b(3)

    step = heads[0]
    tail = heads[2]
    rate = jnp.exp(column(rate_log[...]))
    tail_sum = hsum[2]
    over = jnp.sum(hsum[3], axis=1, keepdims=True)
    cum_end = heads[1][:, TOKENS - 1 :]
    whole = jnp.where(begin_last < 0, jnp.exp(cum_end), 0.0)
    log_grad = (
        nn(hsum[0], not_before.astype(F32), HIGH)
        + nn(tail * step * tail_sum, before.astype(F32), HIGH)
        + heads[4]
        + whole * over
    )
    rate_part = -log_grad * rate * step
    pad = jnp.zeros((TOKENS - 2 * n_heads, TOKENS), F32)
    head_sums = nt(ones, jnp.concatenate([hsum[1], rate_part, pad], axis=0), HIGH)
    pieces = channels // TOKENS

    for n in range(pieces):
        zmsg[n : n + 1] = rows[2:3, n * TOKENS : (n + 1) * TOKENS]
    zmsg[pieces : pieces + 8] = head_sums
    zbuf[z] = zmsg[...]

    def z_copy(n, slot):
        return remote(zmsg, zbuf.at[slot], zss.at[n], zrs.at[slot], {"ctx": z_peers[n]})

    for n in range(Z_SIZE - 1):
        z_copy(n, z).start()

    step_grad = heads[3] / step + tail * tail_sum - rate * log_grad
    shifted = raw[...] + column(bias[...])
    graw[...] = jax.nn.sigmoid(shifted) * step_grad
    for g in range(groups):
        spread = dgram[g].astype(BF16)
        part = slice(g * TOKENS, (g + 1) * TOKENS)
        gc[:, part] = (dc[g] + nn(spread, group(b, g))).astype(BF16)
        gb[:, part] = (db[g] + tn(spread, group(c, g))).astype(BF16)

    for n in range(Z_SIZE - 1):
        z_copy(n, lax.rem(z + n + 1, Z_SIZE)).wait_recv()
    total = zbuf[0]
    for n in range(1, Z_SIZE):
        total = total + zbuf[n]
    xmsg[...] = total
    xbuf[xc] = total

    def x_copy(n, slot):
        return remote(xmsg, xbuf.at[slot], xss.at[n], xrs.at[slot], xc_ids[n])

    for n in range(X_SIZE * CORES - 1):
        x_copy(n, xc).start()
    for n in range(X_SIZE * CORES - 1):
        x_copy(n, xc_peers[n]).wait_recv()
    total = xbuf[0]
    for n in range(1, X_SIZE * CORES):
        total = total + xbuf[n]
    for n in range(pieces):
        ggain[0:1, n * TOKENS : (n + 1) * TOKENS] = total[n : n + 1]
    gskip[...] = total[pieces : pieces + 1, :n_heads]
    grate[...] = total[pieces : pieces + 1, n_heads : 2 * n_heads]

    for hop in range(REACH):
        for copy in kv_copies(hop):
            copy.wait_send()
        for kv in range(KV):
            d_copy(kv, hop).wait_send()
    for copy, chunk in ((f_copy, f_chunk), (b_copy, b_chunk)):
        for stage in range(4):
            for g in range(groups):
                ch = chunk(stage, g)
                copy(0, ch, 0).wait_send()
                if stage < 3:
                    copy(1, ch, 1).wait_send()
    for peer in tp_peers:
        t_copy(peer, tp).wait_send()
    for n in range(Z_SIZE - 1):
        z_copy(n, z).wait_send()
    for n in range(X_SIZE * CORES - 1):
        x_copy(n, xc).wait_send()


def per_device(
    ssm_input, ssm_gate, step_raw, b_proj, c_proj, rate_log, step_bias, skip_gain, norm_gain,
    ssm_grad_out, queries, keys, values, attention_output_gradient, doc_lengths,
):
    channels = ssm_input.shape[2]
    n_heads = rate_log.shape[0]
    groups = b_proj.shape[2] // TOKENS
    chunks = channels // CHUNK
    vmem = pl.BlockSpec(memory_space=pltpu.VMEM)
    smem = pl.BlockSpec(memory_space=pltpu.SMEM)
    wide = jax.ShapeDtypeStruct((TOKENS, channels), BF16)
    narrow = jax.ShapeDtypeStruct((TOKENS, groups * TOKENS), BF16)
    head_row = jax.ShapeDtypeStruct((1, n_heads), F32)
    square = (TOKENS, TOKENS)
    chunked = (chunks, TOKENS, CHUNK)
    window = (REACH + 1) * TOKENS
    message = (channels // TOKENS + 8, TOKENS)
    dma = pltpu.SemaphoreType.DMA
    scratch = [
        pltpu.VMEM((n_heads,) + square, BF16),
        pltpu.VMEM((n_heads,) + square, BF16),
        pltpu.VMEM((TOKENS, channels), F32),
        pltpu.VMEM((TOKENS, channels), BF16),
        pltpu.VMEM((TOKENS, channels), BF16),
        pltpu.VMEM((TOKENS, channels), F32),
        pltpu.VMEM((TOKENS, channels), F32),
        pltpu.VMEM((TOKENS, channels), F32),
        pltpu.VMEM((8, channels), F32),
        pltpu.VMEM((n_heads, channels), BF16),
        pltpu.VMEM((5, n_heads, TOKENS), F32),
        pltpu.VMEM((groups,) + square, F32),
        pltpu.VMEM((groups,) + square, F32),
        pltpu.VMEM(chunked, F32),
        pltpu.VMEM(chunked, F32),
        pltpu.VMEM((2,) + chunked, BF16),
        pltpu.VMEM((2,) + chunked, BF16),
        pltpu.VMEM((2,) + chunked, BF16),
        pltpu.VMEM((2,) + chunked, BF16),
        pltpu.VMEM((REACH, TOKENS, KV * TOKENS), BF16),
        pltpu.VMEM((REACH, TOKENS, KV * TOKENS), BF16),
        pltpu.VMEM((KV, window, TOKENS), BF16),
        pltpu.VMEM((KV, window, TOKENS), BF16),
        pltpu.VMEM((KV, window, 2 * TOKENS), F32),
        pltpu.VMEM((KV, REACH, TOKENS, 2 * TOKENS), BF16),
        pltpu.VMEM((KV, REACH, TOKENS, 2 * TOKENS), BF16),
        pltpu.VMEM((2,) + square, F32),
        pltpu.VMEM((8, TOKENS), F32),
        pltpu.VMEM((TP_SIZE, 8, TOKENS), F32),
        pltpu.VMEM((2,) + square, F32),
        pltpu.VMEM((groups,) + square, F32),
        pltpu.VMEM((groups,) + square, F32),
        pltpu.VMEM((4, n_heads, TOKENS), F32),
        pltpu.VMEM(message, F32),
        pltpu.VMEM((Z_SIZE,) + message, F32),
        pltpu.VMEM(message, F32),
        pltpu.VMEM((X_SIZE * CORES,) + message, F32),
        dma((2, chunks)),
        dma((2, chunks)),
        dma((2, chunks)),
        dma((2, chunks)),
        dma((2, REACH)),
        dma((2, REACH)),
        dma((KV, REACH)),
        dma((KV, REACH)),
        dma((TP_SIZE,)),
        dma((TP_SIZE,)),
        dma((Z_SIZE,)),
        dma((Z_SIZE,)),
        dma((X_SIZE * CORES,)),
        dma((X_SIZE * CORES,)),
    ]
    results = pl.pallas_call(
        kernel,
        out_shape=(
            wide,
            wide,
            jax.ShapeDtypeStruct((n_heads, TOKENS), F32),
            narrow,
            narrow,
            head_row,
            head_row,
            jax.ShapeDtypeStruct((1, channels), F32),
            wide,
            narrow,
            narrow,
        ),
        in_specs=[smem] + [vmem] * 14,
        out_specs=(vmem,) * 11,
        scratch_shapes=scratch,
        compiler_params=pltpu.CompilerParams(
            collective_id=0, has_side_effects=True, vmem_limit_bytes=60 * 1024 * 1024
        ),
        name="mixer_and_attention",
    )(
        doc_lengths,
        ssm_input[0],
        ssm_gate[0],
        step_raw[0],
        b_proj[0],
        c_proj[0],
        rate_log[None],
        step_bias[None],
        skip_gain[None],
        norm_gain[None],
        ssm_grad_out[0],
        queries[0],
        keys[0],
        values[0],
        attention_output_gradient[0],
    )
    gx, ggate, graw, gb, gc, grate, gskip, ggain, gq, gk, gv = results
    return (
        gx[None], ggate[None], graw[None], gb[None], gc[None],
        grate[0], gskip[0], ggain[0], gq[None], gk[None], gv[None],
    )


def solution(mesh):
    tokens = P("dp", "ctx", "tp")
    steps = P("dp", "tp", "ctx")
    param = P("tp")
    return jax.shard_map(
        per_device,
        mesh=mesh,
        in_specs=(
            tokens, tokens, steps, tokens, tokens, param, param, param, param,
            tokens, tokens, tokens, tokens, tokens, P("dp", None),
        ),
        out_specs=(
            tokens, tokens, steps, tokens, tokens, param, param, param,
            tokens, tokens, tokens,
        ),
        check_vma=False,
    )
```

```python
import jax
import jax.numpy as jnp
from jax import lax
from jax.experimental import pallas as pl
from jax.experimental.pallas import tpu as pltpu
from jax.sharding import PartitionSpec as P

MESH = pl.DeviceIdType.MESH
F32 = jnp.float32
BF16 = jnp.bfloat16
HIGH = lax.Precision.HIGHEST

TOKENS = 128
WIDE = 64
REACH = 4
CHUNK = 256
CUT = 64
KV = 2
NORM_WIDTH = 8192
EPSILON = 1e-05
MASKED = -1e30
SCALE = 128.0**-0.5
Z_SIZE = 8
X_SIZE = 4
CORES = 2
VMEM_LIMIT = 62000000
TP_SIZE = 4


def dot(a, b, dims, precision=None):
    return lax.dot_general(
        a, b, (dims, ((), ())), precision=precision, preferred_element_type=F32
    )


def nn(a, b, precision=None):
    return dot(a, b, ((1,), (0,)), precision)


def nt(a, b, precision=None):
    return dot(a, b, ((1,), (1,)), precision)


def tn(a, b, precision=None):
    return dot(a, b, ((0,), (0,)), precision)


def iota(shape, axis):
    return lax.broadcasted_iota(jnp.int32, shape, axis)


def lanes(start, size):
    return pl.ds(pl.multiple_of(start, size), size)


def column(row):
    size = row.shape[1]
    on_diagonal = iota((size, size), 0) == iota((size, size), 1)
    return jnp.sum(jnp.where(on_diagonal, row, 0.0), axis=1, keepdims=True)


def turned(row):
    return jnp.transpose(jnp.broadcast_to(row, (TOKENS, TOKENS)))


def twice(a):
    return jnp.concatenate([a, a], axis=1)


def folded(a):
    return a[:, :TOKENS] + a[:, TOKENS:]


def kernel(
    lens, x_in, gate_in, raw_in, b_in, c_in, rate_log, bias, skip, gain,
    dout_in, q_in, k_in, v_in, do_in,
    gx, ggate, graw, gb, gc, grate, gskip, ggain, gq, gk, gv,
    ls, w, mixed, carried, dy, dxin, sve, tse, rows, marks, heads,
    gram, dgram, loc, dsl, fsend, frecv, bsend, brecv, kw, vw, kall, vall,
    dacc, dsend, drecv, tsum, tmsg, tbuf, cols, dc, db, hsum, zmsg, zbuf, xmsg, xbuf,
    zlate, zlbuf, xlate, xlbuf, x, gate, raw, b, c, dout, q, k, v, do,
    fss, frs, bss, brs, kss, krs, dss, drs, tss, trs, zss, zrs, xss, xrs, ins,
):
    i = lax.axis_index("ctx")
    core = lax.axis_index("dp")
    tp = lax.axis_index("tp")
    count = Z_SIZE * X_SIZE
    right = lax.rem(i + 1, count)
    left = lax.rem(i + count - 1, count)
    z = lax.rem(i, Z_SIZE)
    xi = i // Z_SIZE
    xc = xi * CORES + core
    z_peers = [xi * Z_SIZE + lax.rem(z + n, Z_SIZE) for n in range(1, Z_SIZE)]
    xc_peers = [lax.rem(xc + n, X_SIZE * CORES) for n in range(1, X_SIZE * CORES)]
    xc_ids = [{"ctx": (p // CORES) * Z_SIZE + z, "dp": lax.rem(p, CORES)} for p in xc_peers]
    tp_peers = [lax.rem(tp + n, TP_SIZE) for n in range(1, TP_SIZE)]
    n_heads = raw.shape[0]
    channels = x.shape[1]
    groups = b.shape[1] // TOKENS
    pairs = n_heads // 2 // groups

    barrier = pltpu.get_barrier_semaphore()
    greeted = (
        [{"ctx": left}, {"ctx": right}]
        + [{"tp": p} for p in tp_peers]
        + [{"ctx": p} for p in z_peers]
        + xc_ids
    )
    for device in greeted:
        pl.semaphore_signal(barrier, inc=1, device_id=device, device_id_type=MESH)

    loads = []
    for source, target in (
        (raw_in, raw), (x_in, x), (b_in, b), (c_in, c), (k_in, k), (v_in, v),
        (gate_in, gate), (dout_in, dout), (q_in, q), (do_in, do),
    ):
        loads.append((target, pltpu.make_async_copy(source, target, ins.at[len(loads)])))
        loads[-1][1].start()

    def loaded(*targets):
        for target, load in loads:
            if any(target is wanted for wanted in targets):
                load.wait()

    def remote(source, target, send, recv, device):
        return pltpu.make_async_remote_copy(
            src_ref=source,
            dst_ref=target,
            send_sem=send,
            recv_sem=recv,
            device_id=device,
            device_id_type=MESH,
        )

    def kv_copies(hop):
        slot = REACH - 1 - hop
        k_from = k if hop == 0 else kw.at[slot + 1]
        v_from = v if hop == 0 else vw.at[slot + 1]
        to = {"ctx": right}
        return (
            remote(k_from, kw.at[slot], kss.at[0, hop], krs.at[0, hop], to),
            remote(v_from, vw.at[slot], kss.at[1, hop], krs.at[1, hop], to),
        )

    def kv_start(hop):
        for copy in kv_copies(hop):
            copy.start()

    def kv_wait(hop):
        for copy in kv_copies(hop):
            copy.wait_recv()

    base = i * TOKENS
    position = iota((8, TOKENS), 1) + base
    begin = jnp.zeros((8, TOKENS), jnp.int32)
    end = jnp.int32(0)
    for d in range(lens.shape[1]):
        end = end + lens[0, d]
        begin = begin + jnp.where(position >= end, lens[0, d], 0)
    begin_row = (begin - base)[0:1]
    begin_last = begin_row[:, TOKENS - 1 :]
    begin_col = turned(begin_row.astype(F32))
    row_id = iota((TOKENS, TOKENS), 0)
    lane_id = iota((TOKENS, TOKENS), 1)
    within = (lane_id <= row_id) & (lane_id.astype(F32) >= begin_col)
    up_to = (row_id <= lane_id).astype(F32)

    loaded(raw)
    shifted = raw[...] + column(bias[...])
    step = jax.nn.softplus(shifted)
    rate = jnp.exp(column(rate_log[...]))
    decay = -rate * step
    cum = nn(decay, up_to, HIGH)
    cum_end = cum[:, TOKENS - 1 :]
    survive = jnp.where(begin_row < 0, jnp.exp(cum), 0.0)
    tail = jnp.where(iota((1, TOKENS), 1) >= begin_last, jnp.exp(cum_end - cum), 0.0)
    whole = jnp.where(begin_last < 0, jnp.exp(cum_end), 0.0)
    heads[0] = step
    heads[1] = cum
    heads[2] = tail
    mark = iota((n_heads, channels), 1) // WIDE == iota((n_heads, channels), 0)
    marks[...] = mark.astype(BF16)
    both = jnp.concatenate([marks[...], marks[...]], axis=0)

    def expand(a):
        high = a.astype(BF16)
        low = (a - high.astype(F32)).astype(BF16)
        return tn(jnp.concatenate([high, low], axis=0), both)

    tse[...] = expand(tail * step)
    rows[0:1] = jnp.sum(jnp.where(mark, whole, 0.0), axis=0, keepdims=True)

    def group(a, g):
        return a[:, g * TOKENS : (g + 1) * TOKENS]

    def local_state(ch, g):
        part = lanes(ch * CHUNK, CHUNK)
        inputs = (x[:, part].astype(F32) * tse[:, part]).astype(BF16)
        loc[ch] = tn(group(b, g), inputs)

    def f_chunk(stage, g):
        return g * 4 + lax.rem(stage + 4 * count - i, 4)

    def b_chunk(stage, g):
        return g * 4 + lax.rem(stage + i, 4)

    def chain(send, recv, ss, rs, device):
        def copy(leg, ch, to, n):
            cut = slice(n * CUT, (n + 1) * CUT)
            return remote(
                send.at[leg, ch, cut], recv.at[to, ch, cut],
                ss.at[leg, ch, n], rs.at[to, ch, n], device,
            )

        return copy

    f_copy = chain(fsend, frecv, fss, frs, {"ctx": right})
    b_copy = chain(bsend, brecv, bss, brs, {"ctx": left})

    def leg_a(copy, send, recv, own, ch, stage):
        for n in range(TOKENS // CUT):
            cut = slice(n * CUT, (n + 1) * CUT)
            value = own[ch, cut]
            if stage > 0:
                copy(0, ch, 0, n).wait_recv()
                decayed = rows[0:1, lanes(ch * CHUNK, CHUNK)] * recv[0, ch, cut].astype(F32)
                value = value + decayed
            send[0, ch, cut] = value.astype(BF16)
            copy(0, ch, 1 if stage == 3 else 0, n).start()

    def leg_b(copy, send, recv, own, ch, stage):
        for n in range(TOKENS // CUT):
            cut = slice(n * CUT, (n + 1) * CUT)
            copy(1, ch, 1, n).wait_recv()
            if stage < 3:
                decayed = rows[0:1, lanes(ch * CHUNK, CHUNK)] * recv[1, ch, cut].astype(F32)
                send[1, ch, cut] = (own[ch, cut] + decayed).astype(BF16)
                copy(1, ch, 1, n).start()

    def f_leg_a(stage):
        for g in range(groups):
            leg_a(f_copy, fsend, frecv, loc, f_chunk(stage, g), stage)

    def b_leg_a(stage):
        for g in range(groups):
            leg_a(b_copy, bsend, brecv, dsl, b_chunk(stage, g), stage)

    loaded(x, b)
    for g in range(groups):
        local_state(f_chunk(0, g), g)
    pl.semaphore_wait(barrier, len(greeted))
    f_leg_a(0)
    loaded(k, v)
    kv_start(0)
    for stage in range(1, 4):
        for g in range(groups):
            local_state(f_chunk(stage, g), g)
    sve[...] = expand(survive)
    rows[1:2] = jnp.sum(jnp.where(mark, column(skip[...]), 0.0), axis=0, keepdims=True)
    loaded(c)
    for g in range(groups):
        gram[g] = nt(group(c, g), group(b, g))

    left_half = iota((1, TOKENS), 1) < WIDE

    def inside_pair(g, first, last):
        def body(n, _):
            pair = g * pairs + n
            part = lanes(pair * TOKENS, TOKENS)
            for e in range(2):
                h = pair * 2 + e
                cum_row = heads[1, pl.ds(h, 1), :]
                gap = jnp.where(within, turned(cum_row) - cum_row, MASKED)
                scaled = jnp.exp(gap) * heads[0, pl.ds(h, 1), :]
                ls[h] = scaled.astype(BF16)
                w[h] = (scaled * gram[g]).astype(BF16)
            x_part = x[:, part]
            product = nn(w[pl.ds(pair * 2, 2)].reshape(2 * TOKENS, TOKENS), x_part)
            inside = jnp.where(left_half, product[:TOKENS], product[TOKENS:])
            mixed[:, part] = inside + rows[1:2, part] * x_part.astype(F32)
            return 0

        lax.fori_loop(first, last, body, 0)

    def attention(kv, first, last):
        key = kall[kv]
        value = vall[kv]
        window = (REACH + 1) * TOKENS
        key_at = iota((window, 2 * TOKENS), 0) - REACH * TOKENS
        query_at = twice(iota((1, TOKENS), 1))
        allowed = (key_at <= query_at) & (key_at >= twice(begin_row))

        def body(n, _):
            offset = (kv * 4 + n) * 2 * TOKENS
            part = lanes(offset, 2 * TOKENS)
            q_two = q[:, part]
            do_two = do[:, part]
            query = jnp.concatenate([q_two[:, :TOKENS], q_two[:, TOKENS:]], axis=0)
            cotangent = jnp.concatenate([do_two[:, :TOKENS], do_two[:, TOKENS:]], axis=0)
            score = jnp.where(allowed, nt(key, query) * SCALE, MASKED)
            top = jnp.max(score, axis=0, keepdims=True)
            weight = jnp.exp(score - top)
            total = jnp.sum(weight, axis=0, keepdims=True)
            prob = weight * (1.0 / total)
            reply = nt(value, cotangent)
            centre = jnp.sum(prob * reply, axis=0, keepdims=True)
            score_grad = (prob * (reply - centre)).astype(BF16)
            query_grad = (tn(score_grad, key) * SCALE).astype(BF16)
            gq[:, part] = jnp.concatenate([query_grad[:TOKENS], query_grad[TOKENS:]], axis=1)
            dacc[kv, :, 0:TOKENS] += nn(score_grad, query) * SCALE
            dacc[kv, :, TOKENS : 2 * TOKENS] += nn(prob.astype(BF16), cotangent)
            return 0

        lax.fori_loop(first, last, body, 0)

    def d_copy(kv, hop):
        return remote(
            dsend.at[kv, hop], drecv.at[kv, hop], dss.at[kv, hop], drs.at[kv, hop], {"ctx": left}
        )

    def d_hop(kv, hop):
        own = dacc[kv, hop * TOKENS : (hop + 1) * TOKENS]
        if hop > 0:
            d_copy(kv, hop - 1).wait_recv()
            own = own + drecv[kv, hop - 1].astype(F32)
        if hop < REACH:
            dsend[kv, hop] = own.astype(BF16)
            d_copy(kv, hop).start()
        else:
            gk[:, kv * TOKENS : (kv + 1) * TOKENS] = own[:, :TOKENS].astype(BF16)
            gv[:, kv * TOKENS : (kv + 1) * TOKENS] = own[:, TOKENS:].astype(BF16)

    def gating(part):
        g_here = gate[:, part].astype(F32)
        sigma = jax.nn.sigmoid(g_here)
        activation = g_here * sigma
        out_grad = dout[:, part].astype(F32)
        return g_here, sigma, activation, out_grad, out_grad * gain[0:1, part]

    def middle(ch, g):
        part = lanes(ch * CHUNK, CHUNK)
        entered = nn(group(c, g), frecv[1, ch]) * sve[:, part]
        carried[:, part] = entered.astype(BF16)
        here = mixed[:, part] + entered
        mixed[:, part] = here
        _, _, activation, _, scaled = gating(part)
        gated = here * activation
        tsum[0] += folded(gated * gated)
        tsum[1] += folded(gated * scaled)

    def f_leg_b(stage):
        for g in range(groups):
            leg_b(f_copy, fsend, frecv, loc, f_chunk(stage, g), stage)

    def f_middle(stage):
        for g in range(groups):
            middle(f_chunk(stage, g), g)

    tsum[...] = jnp.zeros_like(tsum)
    dacc[...] = jnp.zeros_like(dacc)
    dgram[...] = jnp.zeros_like(dgram)
    dc[...] = jnp.zeros_like(dc)
    db[...] = jnp.zeros_like(db)
    hsum[...] = jnp.zeros_like(hsum)

    def gather_window():
        for kv in range(KV):
            head = slice(kv * TOKENS, (kv + 1) * TOKENS)
            for slot in range(REACH + 1):
                window = slice(slot * TOKENS, (slot + 1) * TOKENS)
                kall[kv, window] = kw[slot, :, head] if slot < REACH else k[:, head]
                vall[kv, window] = vw[slot, :, head] if slot < REACH else v[:, head]

    f_leg_a(1)
    inside_pair(0, 0, 8)
    f_leg_a(2)
    inside_pair(1, 0, 8)
    f_leg_a(3)
    kv_wait(0)
    kv_start(1)
    loaded(gate, dout, q, do)
    f_leg_b(0)
    f_middle(0)
    f_leg_b(1)
    f_middle(1)
    f_leg_b(2)
    f_middle(2)
    f_leg_b(3)
    kv_wait(1)
    kv_start(2)
    f_middle(3)

    ones = jnp.ones((8, TOKENS), F32)
    squares = nt(ones, tsum[0], HIGH)
    crosses = nt(ones, tsum[1], HIGH)
    message = jnp.where(iota((8, TOKENS), 0) == 0, squares, crosses)
    tmsg[...] = message
    tbuf[tp] = message

    def t_copy(peer, slot):
        return remote(tmsg, tbuf.at[slot], tss.at[peer], trs.at[slot], {"tp": peer})

    for peer in tp_peers:
        t_copy(peer, tp).start()
    for peer in tp_peers:
        t_copy(peer, peer).wait_recv()
    total = tbuf[0] + tbuf[1] + tbuf[2] + tbuf[3]
    factor = lax.rsqrt(total[0:1] / NORM_WIDTH + EPSILON)
    pull = factor * factor * factor * total[1:2] / NORM_WIDTH
    cols[0] = turned(factor)
    cols[1] = turned(pull)

    def cotangents(ch, g):
        part = lanes(ch * CHUNK, CHUNK)
        g_here, sigma, activation, out_grad, scaled = gating(part)
        here = mixed[:, part]
        gated = here * activation
        factor_col = twice(cols[0])
        gated_grad = factor_col * scaled - gated * twice(cols[1])
        mixed_grad = gated_grad * activation
        dy[:, part] = mixed_grad.astype(BF16)
        dsl[ch] = tn(group(c, g), (mixed_grad * sve[:, part]).astype(BF16))
        gate_grad = gated_grad * here * sigma * (1.0 + g_here * (1.0 - sigma))
        ggate[:, part] = gate_grad.astype(BF16)
        rows[2:3, part] = jnp.sum(out_grad * gated * factor_col, axis=0, keepdims=True)

    def side_sums(ch, g):
        part = lanes(ch * CHUNK, CHUNK)
        mixed_grad = dy[:, part].astype(F32)
        mark_part = marks[:, part]
        dc[g] += nt((mixed_grad * sve[:, part]).astype(BF16), frecv[1, ch])
        hsum[0] += nt(mark_part, (mixed_grad * carried[:, part].astype(F32)).astype(BF16))
        hsum[1] += nt(mark_part, (mixed_grad * x[:, part].astype(F32)).astype(BF16))

    for g in range(groups):
        cotangents(b_chunk(0, g), g)
    b_leg_a(0)
    for stage in range(1, 4):
        for g in range(groups):
            cotangents(b_chunk(stage, g), g)

    before = (row_id < lane_id).astype(BF16)
    not_before = row_id >= lane_id

    def inside_back(g, first, last):
        def body(n, _):
            pair = g * pairs + n
            part = lanes(pair * TOKENS, TOKENS)
            dy_part = dy[:, part]
            zero = jnp.zeros_like(dy_part)
            split = jnp.concatenate(
                [jnp.where(left_half, dy_part, zero), jnp.where(left_half, zero, dy_part)], axis=0
            )
            weight_grad = nt(split, x[:, part])
            w_two = w[pl.ds(pair * 2, 2)].reshape(2 * TOKENS, TOKENS)
            ls_two = ls[pl.ds(pair * 2, 2)].reshape(2 * TOKENS, TOKENS)
            spread = weight_grad * ls_two.astype(F32)
            dgram[g] += spread[:TOKENS] + spread[TOKENS:]
            moment = weight_grad * w_two.astype(F32)
            crossing = nn(moment.astype(BF16), before)
            for e in range(2):
                half = slice(e * TOKENS, (e + 1) * TOKENS)
                row = pl.ds(pair * 2 + e, 1)
                heads[3, row, :] = jnp.sum(moment[half], axis=0, keepdims=True)
                heads[4, row, :] = jnp.sum(
                    jnp.where(not_before, crossing[half], 0.0), axis=0, keepdims=True
                )
            dxin[:, part] = tn(w_two, split)
            return 0

        lax.fori_loop(first, last, body, 0)

    def tail_rates(ch, g):
        part = lanes(ch * CHUNK, CHUNK)
        later = brecv[1, ch]
        mark_part = marks[:, part]
        scaled_grad = nn(group(b, g), later)
        hsum[2] += nt(mark_part, (x[:, part].astype(F32) * scaled_grad).astype(BF16))
        hsum[3] += nt(mark_part, (later.astype(F32) * frecv[1, ch].astype(F32)).astype(BF16))
        dxin[:, part] += rows[1:2, part] * dy[:, part].astype(F32) + scaled_grad * tse[:, part]

    def finish(ch, g):
        part = lanes(ch * CHUNK, CHUNK)
        gx[:, part] = dxin[:, part].astype(BF16)
        db[g] += nt((x[:, part].astype(F32) * tse[:, part]).astype(BF16), brecv[1, ch])

    def b_leg_b(stage):
        for g in range(groups):
            leg_b(b_copy, bsend, brecv, dsl, b_chunk(stage, g), stage)

    def at_stage(work, stage):
        for g in range(groups):
            work(b_chunk(stage, g), g)

    pieces = channels // TOKENS
    z_refs = ((zmsg, zbuf), (zlate, zlbuf))
    x_refs = ((xmsg, xbuf), (xlate, xlbuf))

    def padded(a):
        return jnp.concatenate([a, jnp.zeros((TOKENS - a.shape[0], TOKENS), F32)], axis=0)

    def z_copy(turn, n, slot):
        message, slots = z_refs[turn]
        return remote(
            message, slots.at[slot], zss.at[turn, n], zrs.at[turn, slot], {"ctx": z_peers[n]}
        )

    def x_copy(turn, n, slot):
        message, slots = x_refs[turn]
        return remote(message, slots.at[slot], xss.at[turn, n], xrs.at[turn, slot], xc_ids[n])

    def z_start(turn):
        message, slots = z_refs[turn]
        slots[z] = message[...]
        for n in range(Z_SIZE - 1):
            z_copy(turn, n, z).start()

    def x_start(turn):
        slots = z_refs[turn][1]
        for n in range(Z_SIZE - 1):
            z_copy(turn, n, lax.rem(z + n + 1, Z_SIZE)).wait_recv()
        total = slots[0]
        for n in range(1, Z_SIZE):
            total = total + slots[n]
        message, slots = x_refs[turn]
        message[...] = total
        slots[xc] = total
        for n in range(X_SIZE * CORES - 1):
            x_copy(turn, n, xc).start()

    def x_total(turn):
        slots = x_refs[turn][1]
        for n in range(X_SIZE * CORES - 1):
            x_copy(turn, n, xc_peers[n]).wait_recv()
        total = slots[0]
        for n in range(1, X_SIZE * CORES):
            total = total + slots[n]
        return total

    def early_sums():
        for n in range(pieces):
            zmsg[n : n + 1] = rows[2:3, n * TOKENS : (n + 1) * TOKENS]
        zmsg[pieces : pieces + 8] = nt(ones, padded(hsum[1]), HIGH)
        z_start(0)

    kv_wait(2)
    kv_start(3)
    inside_back(0, 0, pairs)
    b_leg_a(1)
    kv_wait(3)
    gather_window()
    attention(0, 0, 2)
    b_leg_a(2)
    attention(0, 2, 4)
    b_leg_a(3)
    d_hop(0, 0)
    attention(1, 0, 2)
    b_leg_b(0)
    d_hop(0, 1)
    attention(1, 2, 4)
    b_leg_b(1)
    d_hop(1, 0)
    inside_back(1, 0, pairs)
    d_hop(0, 2)
    b_leg_b(2)
    for stage in range(3):
        at_stage(tail_rates, stage)
    for stage in range(4):
        at_stage(side_sums, stage)
    early_sums()
    d_hop(1, 1)
    d_hop(0, 3)
    b_leg_b(3)
    at_stage(tail_rates, 3)

    step = heads[0]
    tail = heads[2]
    rate = jnp.exp(column(rate_log[...]))
    tail_sum = hsum[2]
    over = jnp.sum(hsum[3], axis=1, keepdims=True)
    cum_end = heads[1][:, TOKENS - 1 :]
    whole = jnp.where(begin_last < 0, jnp.exp(cum_end), 0.0)
    log_grad = (
        nn(hsum[0], not_before.astype(F32), HIGH)
        + nn(tail * step * tail_sum, before.astype(F32), HIGH)
        + heads[4]
        + whole * over
    )
    rate_part = -log_grad * rate * step
    zlate[...] = nt(ones, padded(rate_part), HIGH)
    z_start(1)
    d_hop(1, 2)
    for stage in range(4):
        at_stage(finish, stage)
    d_hop(0, 4)
    x_start(0)
    d_hop(1, 3)

    step_grad = heads[3] / step + tail * tail_sum - rate * log_grad
    shifted = raw[...] + column(bias[...])
    graw[...] = jax.nn.sigmoid(shifted) * step_grad
    for g in range(groups):
        spread = dgram[g].astype(BF16)
        part = slice(g * TOKENS, (g + 1) * TOKENS)
        gc[:, part] = (dc[g] + nn(spread, group(b, g))).astype(BF16)
        gb[:, part] = (db[g] + tn(spread, group(c, g))).astype(BF16)

    x_start(1)
    d_hop(1, 4)
    total = x_total(0)
    for n in range(pieces):
        ggain[0:1, n * TOKENS : (n + 1) * TOKENS] = total[n : n + 1]
    gskip[...] = total[pieces : pieces + 1, :n_heads]
    total = x_total(1)
    grate[...] = total[0:1, :n_heads]

    for hop in range(REACH):
        for copy in kv_copies(hop):
            copy.wait_send()
        for kv in range(KV):
            d_copy(kv, hop).wait_send()
    for copy, chunk in ((f_copy, f_chunk), (b_copy, b_chunk)):
        for stage in range(4):
            for g in range(groups):
                ch = chunk(stage, g)
                for n in range(TOKENS // CUT):
                    copy(0, ch, 0, n).wait_send()
                    if stage < 3:
                        copy(1, ch, 1, n).wait_send()
    for peer in tp_peers:
        t_copy(peer, tp).wait_send()
    for turn in range(2):
        for n in range(Z_SIZE - 1):
            z_copy(turn, n, z).wait_send()
        for n in range(X_SIZE * CORES - 1):
            x_copy(turn, n, xc).wait_send()


def hand_over(*refs):
    results, outputs, sems = refs[:11], refs[11:22], refs[22]
    copies = [
        pltpu.make_async_copy(result, output, sems.at[n])
        for n, (result, output) in enumerate(zip(results, outputs))
    ]
    for copy in copies:
        copy.start()
    for copy in copies:
        copy.wait()


def per_device(
    ssm_input, ssm_gate, step_raw, b_proj, c_proj, rate_log, step_bias, skip_gain, norm_gain,
    ssm_grad_out, queries, keys, values, attention_output_gradient, doc_lengths,
):
    channels = ssm_input.shape[2]
    n_heads = rate_log.shape[0]
    groups = b_proj.shape[2] // TOKENS
    chunks = channels // CHUNK
    vmem = pl.BlockSpec(memory_space=pltpu.VMEM)
    hbm = pl.BlockSpec(memory_space=pltpu.HBM)
    anywhere = pl.BlockSpec(memory_space=pl.ANY)
    smem = pl.BlockSpec(memory_space=pltpu.SMEM)
    wide = jax.ShapeDtypeStruct((TOKENS, channels), BF16)
    narrow = jax.ShapeDtypeStruct((TOKENS, groups * TOKENS), BF16)
    head_row = jax.ShapeDtypeStruct((1, n_heads), F32)
    square = (TOKENS, TOKENS)
    chunked = (chunks, TOKENS, CHUNK)
    window = (REACH + 1) * TOKENS
    message = (channels // TOKENS + 8, TOKENS)
    dma = pltpu.SemaphoreType.DMA
    scratch = [
        pltpu.VMEM((n_heads,) + square, BF16),
        pltpu.VMEM((n_heads,) + square, BF16),
        pltpu.VMEM((TOKENS, channels), F32),
        pltpu.VMEM((TOKENS, channels), BF16),
        pltpu.VMEM((TOKENS, channels), BF16),
        pltpu.VMEM((TOKENS, channels), F32),
        pltpu.VMEM((TOKENS, channels), F32),
        pltpu.VMEM((TOKENS, channels), F32),
        pltpu.VMEM((8, channels), F32),
        pltpu.VMEM((n_heads, channels), BF16),
        pltpu.VMEM((5, n_heads, TOKENS), F32),
        pltpu.VMEM((groups,) + square, F32),
        pltpu.VMEM((groups,) + square, F32),
        pltpu.VMEM(chunked, F32),
        pltpu.VMEM(chunked, F32),
        pltpu.VMEM((2,) + chunked, BF16),
        pltpu.VMEM((2,) + chunked, BF16),
        pltpu.VMEM((2,) + chunked, BF16),
        pltpu.VMEM((2,) + chunked, BF16),
        pltpu.VMEM((REACH, TOKENS, KV * TOKENS), BF16),
        pltpu.VMEM((REACH, TOKENS, KV * TOKENS), BF16),
        pltpu.VMEM((KV, window, TOKENS), BF16),
        pltpu.VMEM((KV, window, TOKENS), BF16),
        pltpu.VMEM((KV, window, 2 * TOKENS), F32),
        pltpu.VMEM((KV, REACH, TOKENS, 2 * TOKENS), BF16),
        pltpu.VMEM((KV, REACH, TOKENS, 2 * TOKENS), BF16),
        pltpu.VMEM((2,) + square, F32),
        pltpu.VMEM((8, TOKENS), F32),
        pltpu.VMEM((TP_SIZE, 8, TOKENS), F32),
        pltpu.VMEM((2,) + square, F32),
        pltpu.VMEM((groups,) + square, F32),
        pltpu.VMEM((groups,) + square, F32),
        pltpu.VMEM((4, n_heads, TOKENS), F32),
        pltpu.VMEM(message, F32),
        pltpu.VMEM((Z_SIZE,) + message, F32),
        pltpu.VMEM(message, F32),
        pltpu.VMEM((X_SIZE * CORES,) + message, F32),
        pltpu.VMEM((8, TOKENS), F32),
        pltpu.VMEM((Z_SIZE, 8, TOKENS), F32),
        pltpu.VMEM((8, TOKENS), F32),
        pltpu.VMEM((X_SIZE * CORES, 8, TOKENS), F32),
        pltpu.VMEM(wide.shape, BF16),
        pltpu.VMEM(wide.shape, BF16),
        pltpu.VMEM((n_heads, TOKENS), F32),
        pltpu.VMEM(narrow.shape, BF16),
        pltpu.VMEM(narrow.shape, BF16),
        pltpu.VMEM(wide.shape, BF16),
        pltpu.VMEM(wide.shape, BF16),
        pltpu.VMEM(narrow.shape, BF16),
        pltpu.VMEM(narrow.shape, BF16),
        pltpu.VMEM(wide.shape, BF16),
        dma((2, chunks, TOKENS // CUT)),
        dma((2, chunks, TOKENS // CUT)),
        dma((2, chunks, TOKENS // CUT)),
        dma((2, chunks, TOKENS // CUT)),
        dma((2, REACH)),
        dma((2, REACH)),
        dma((KV, REACH)),
        dma((KV, REACH)),
        dma((TP_SIZE,)),
        dma((TP_SIZE,)),
        dma((2, Z_SIZE)),
        dma((2, Z_SIZE)),
        dma((2, X_SIZE * CORES)),
        dma((2, X_SIZE * CORES)),
        dma((10,)),
    ]
    shapes = (
        wide, wide, jax.ShapeDtypeStruct((n_heads, TOKENS), F32), narrow, narrow, head_row,
        head_row, jax.ShapeDtypeStruct((1, channels), F32), wide, narrow, narrow,
    )
    results = pl.pallas_call(
        kernel,
        out_shape=shapes,
        in_specs=[smem] + [hbm] * 5 + [vmem] * 4 + [hbm] * 5,
        out_specs=(vmem,) * 11,
        scratch_shapes=scratch,
        compiler_params=pltpu.CompilerParams(
            collective_id=0, has_side_effects=True, vmem_limit_bytes=VMEM_LIMIT
        ),
        name="mixer_and_attention",
    )(
        doc_lengths,
        ssm_input[0],
        ssm_gate[0],
        step_raw[0],
        b_proj[0],
        c_proj[0],
        rate_log[None],
        step_bias[None],
        skip_gain[None],
        norm_gain[None],
        ssm_grad_out[0],
        queries[0],
        keys[0],
        values[0],
        attention_output_gradient[0],
    )
    results = pl.pallas_call(
        hand_over,
        out_shape=shapes,
        in_specs=[vmem] * 11,
        out_specs=(anywhere,) * 11,
        scratch_shapes=[dma((11,))],
        compiler_params=pltpu.CompilerParams(vmem_limit_bytes=VMEM_LIMIT),
        name="hand_over",
    )(*results)
    gx, ggate, graw, gb, gc, grate, gskip, ggain, gq, gk, gv = results
    return (
        gx[None], ggate[None], graw[None], gb[None], gc[None],
        grate[0], gskip[0], ggain[0], gq[None], gk[None], gv[None],
    )


def solution(mesh):
    tokens = P("dp", "ctx", "tp")
    steps = P("dp", "tp", "ctx")
    param = P("tp")
    return jax.shard_map(
        per_device,
        mesh=mesh,
        in_specs=(
            tokens, tokens, steps, tokens, tokens, param, param, param, param,
            tokens, tokens, tokens, tokens, tokens, P("dp", None),
        ),
        out_specs=(
            tokens, tokens, steps, tokens, tokens, param, param, param,
            tokens, tokens, tokens,
        ),
        check_vma=False,
    )
```

```python
import jax
import jax.numpy as jnp
from jax import lax
from jax.experimental import pallas as pl
from jax.experimental.pallas import tpu as pltpu
from jax.sharding import PartitionSpec as P

MESH = pl.DeviceIdType.MESH
F32 = jnp.float32
BF16 = jnp.bfloat16
HIGH = lax.Precision.HIGHEST

TOKENS = 128
WIDE = 64
REACH = 4
CHUNK = 256
CUT = 64
KV = 2
NORM_WIDTH = 8192
EPSILON = 1e-05
MASKED = -1e30
SCALE = 128.0**-0.5
Z_SIZE = 8
X_SIZE = 4
CORES = 2
VMEM_LIMIT = 62000000
TP_SIZE = 4


def dot(a, b, dims, precision=None):
    return lax.dot_general(
        a, b, (dims, ((), ())), precision=precision, preferred_element_type=F32
    )


def nn(a, b, precision=None):
    return dot(a, b, ((1,), (0,)), precision)


def nt(a, b, precision=None):
    return dot(a, b, ((1,), (1,)), precision)


def tn(a, b, precision=None):
    return dot(a, b, ((0,), (0,)), precision)


def iota(shape, axis):
    return lax.broadcasted_iota(jnp.int32, shape, axis)


def lanes(start, size):
    return pl.ds(pl.multiple_of(start, size), size)


def column(row):
    size = row.shape[1]
    on_diagonal = iota((size, size), 0) == iota((size, size), 1)
    return jnp.sum(jnp.where(on_diagonal, row, 0.0), axis=1, keepdims=True)


def turned(row):
    return jnp.transpose(jnp.broadcast_to(row, (TOKENS, TOKENS)))


def twice(a):
    return jnp.concatenate([a, a], axis=1)


def folded(a):
    return a[:, :TOKENS] + a[:, TOKENS:]


def kernel(
    lens, x_in, gate_in, raw_in, b_in, c_in, rate_log, bias, skip, gain,
    dout_in, q_in, k_in, v_in, do_in,
    gx_out, ggate_out, graw, gb, gc, grate, gskip, ggain, gq_out, gk, gv,
    ls, w, mixed, carried, dy, dxin, sve, tse, rows, marks, heads,
    gram, dgram, loc, dsl, fsend, frecv, bsend, brecv, kw, vw, kall, vall,
    dacc, dsend, drecv, tsum, tmsg, tbuf, cols, dc, db, hsum, zmsg, zbuf, xmsg, xbuf,
    zlate, zlbuf, xlate, xlbuf, x, gate, raw, b, c, dout, q, k, v, do,
    gx, ggate, gq, fss, frs, bss, brs, kss, krs, dss, drs, tss, trs, zss, zrs, xss, xrs, ins, outs,
):
    i = lax.axis_index("ctx")
    core = lax.axis_index("dp")
    tp = lax.axis_index("tp")
    count = Z_SIZE * X_SIZE
    right = lax.rem(i + 1, count)
    left = lax.rem(i + count - 1, count)
    z = lax.rem(i, Z_SIZE)
    xi = i // Z_SIZE
    xc = xi * CORES + core
    z_peers = [xi * Z_SIZE + lax.rem(z + n, Z_SIZE) for n in range(1, Z_SIZE)]
    xc_peers = [lax.rem(xc + n, X_SIZE * CORES) for n in range(1, X_SIZE * CORES)]
    xc_ids = [{"ctx": (p // CORES) * Z_SIZE + z, "dp": lax.rem(p, CORES)} for p in xc_peers]
    tp_peers = [lax.rem(tp + n, TP_SIZE) for n in range(1, TP_SIZE)]
    n_heads = raw.shape[0]
    channels = x.shape[1]
    groups = b.shape[1] // TOKENS
    pairs = n_heads // 2 // groups

    barrier = pltpu.get_barrier_semaphore()
    greeted = (
        [{"ctx": left}, {"ctx": right}]
        + [{"tp": p} for p in tp_peers]
        + [{"ctx": p} for p in z_peers]
        + xc_ids
    )
    for device in greeted:
        pl.semaphore_signal(barrier, inc=1, device_id=device, device_id_type=MESH)

    loads = []
    for source, target in (
        (raw_in, raw), (x_in, x), (b_in, b), (c_in, c), (k_in, k), (v_in, v),
        (gate_in, gate), (dout_in, dout), (q_in, q), (do_in, do),
    ):
        loads.append((target, pltpu.make_async_copy(source, target, ins.at[len(loads)])))
        loads[-1][1].start()

    def loaded(*targets):
        for target, load in loads:
            if any(target is wanted for wanted in targets):
                load.wait()

    def remote(source, target, send, recv, device):
        return pltpu.make_async_remote_copy(
            src_ref=source,
            dst_ref=target,
            send_sem=send,
            recv_sem=recv,
            device_id=device,
            device_id_type=MESH,
        )

    def kv_copies(hop):
        slot = REACH - 1 - hop
        k_from = k if hop == 0 else kw.at[slot + 1]
        v_from = v if hop == 0 else vw.at[slot + 1]
        to = {"ctx": right}
        return (
            remote(k_from, kw.at[slot], kss.at[0, hop], krs.at[0, hop], to),
            remote(v_from, vw.at[slot], kss.at[1, hop], krs.at[1, hop], to),
        )

    def kv_start(hop):
        for copy in kv_copies(hop):
            copy.start()

    def kv_wait(hop):
        for copy in kv_copies(hop):
            copy.wait_recv()

    base = i * TOKENS
    position = iota((8, TOKENS), 1) + base
    begin = jnp.zeros((8, TOKENS), jnp.int32)
    end = jnp.int32(0)
    for d in range(lens.shape[1]):
        end = end + lens[0, d]
        begin = begin + jnp.where(position >= end, lens[0, d], 0)
    begin_row = (begin - base)[0:1]
    begin_last = begin_row[:, TOKENS - 1 :]
    begin_col = turned(begin_row.astype(F32))
    row_id = iota((TOKENS, TOKENS), 0)
    lane_id = iota((TOKENS, TOKENS), 1)
    within = (lane_id <= row_id) & (lane_id.astype(F32) >= begin_col)
    up_to = (row_id <= lane_id).astype(F32)

    loaded(raw)
    shifted = raw[...] + column(bias[...])
    step = jax.nn.softplus(shifted)
    rate = jnp.exp(column(rate_log[...]))
    decay = -rate * step
    cum = nn(decay, up_to, HIGH)
    cum_end = cum[:, TOKENS - 1 :]
    survive = jnp.where(begin_row < 0, jnp.exp(cum), 0.0)
    tail = jnp.where(iota((1, TOKENS), 1) >= begin_last, jnp.exp(cum_end - cum), 0.0)
    whole = jnp.where(begin_last < 0, jnp.exp(cum_end), 0.0)
    heads[0] = step
    heads[1] = cum
    heads[2] = tail
    mark = iota((n_heads, channels), 1) // WIDE == iota((n_heads, channels), 0)
    marks[...] = mark.astype(BF16)
    both = jnp.concatenate([marks[...], marks[...]], axis=0)

    def expand(a):
        high = a.astype(BF16)
        low = (a - high.astype(F32)).astype(BF16)
        return tn(jnp.concatenate([high, low], axis=0), both)

    tse[...] = expand(tail * step)
    rows[0:1] = jnp.sum(jnp.where(mark, whole, 0.0), axis=0, keepdims=True)

    def group(a, g):
        return a[:, g * TOKENS : (g + 1) * TOKENS]

    def local_state(ch, g):
        part = lanes(ch * CHUNK, CHUNK)
        inputs = (x[:, part].astype(F32) * tse[:, part]).astype(BF16)
        loc[ch] = tn(group(b, g), inputs)

    def f_chunk(stage, g):
        return g * 4 + lax.rem(stage + 4 * count - i, 4)

    def b_chunk(stage, g):
        return g * 4 + lax.rem(stage + i, 4)

    def chain(send, recv, ss, rs, device):
        def copy(leg, ch, to, n):
            cut = slice(n * CUT, (n + 1) * CUT)
            return remote(
                send.at[leg, ch, cut], recv.at[to, ch, cut],
                ss.at[leg, ch, n], rs.at[to, ch, n], device,
            )

        return copy

    f_copy = chain(fsend, frecv, fss, frs, {"ctx": right})
    b_copy = chain(bsend, brecv, bss, brs, {"ctx": left})

    def leg_a(copy, send, recv, own, ch, stage):
        for n in range(TOKENS // CUT):
            cut = slice(n * CUT, (n + 1) * CUT)
            value = own[ch, cut]
            if stage > 0:
                copy(0, ch, 0, n).wait_recv()
                decayed = rows[0:1, lanes(ch * CHUNK, CHUNK)] * recv[0, ch, cut].astype(F32)
                value = value + decayed
            send[0, ch, cut] = value.astype(BF16)
            copy(0, ch, 1 if stage == 3 else 0, n).start()

    def leg_b(copy, send, recv, own, ch, stage):
        for n in range(TOKENS // CUT):
            cut = slice(n * CUT, (n + 1) * CUT)
            copy(1, ch, 1, n).wait_recv()
            if stage < 3:
                decayed = rows[0:1, lanes(ch * CHUNK, CHUNK)] * recv[1, ch, cut].astype(F32)
                send[1, ch, cut] = (own[ch, cut] + decayed).astype(BF16)
                copy(1, ch, 1, n).start()

    def f_leg_a(stage):
        for g in range(groups):
            leg_a(f_copy, fsend, frecv, loc, f_chunk(stage, g), stage)

    def b_leg_a(stage):
        for g in range(groups):
            leg_a(b_copy, bsend, brecv, dsl, b_chunk(stage, g), stage)

    loaded(x, b)
    for g in range(groups):
        local_state(f_chunk(0, g), g)
    pl.semaphore_wait(barrier, len(greeted))
    f_leg_a(0)
    loaded(k, v)
    kv_start(0)
    for stage in range(1, 4):
        for g in range(groups):
            local_state(f_chunk(stage, g), g)
    sve[...] = expand(survive)
    rows[1:2] = jnp.sum(jnp.where(mark, column(skip[...]), 0.0), axis=0, keepdims=True)
    loaded(c)
    for g in range(groups):
        gram[g] = nt(group(c, g), group(b, g))

    left_half = iota((1, TOKENS), 1) < WIDE

    def inside_pair(g, first, last):
        def body(n, _):
            pair = g * pairs + n
            part = lanes(pair * TOKENS, TOKENS)
            for e in range(2):
                h = pair * 2 + e
                cum_row = heads[1, pl.ds(h, 1), :]
                gap = jnp.where(within, turned(cum_row) - cum_row, MASKED)
                scaled = jnp.exp(gap) * heads[0, pl.ds(h, 1), :]
                ls[h] = scaled.astype(BF16)
                w[h] = (scaled * gram[g]).astype(BF16)
            x_part = x[:, part]
            product = nn(w[pl.ds(pair * 2, 2)].reshape(2 * TOKENS, TOKENS), x_part)
            inside = jnp.where(left_half, product[:TOKENS], product[TOKENS:])
            mixed[:, part] = inside + rows[1:2, part] * x_part.astype(F32)
            return 0

        lax.fori_loop(first, last, body, 0)

    def attention(kv, first, last):
        key = kall[kv]
        value = vall[kv]
        window = (REACH + 1) * TOKENS
        key_at = iota((window, 2 * TOKENS), 0) - REACH * TOKENS
        query_at = twice(iota((1, TOKENS), 1))
        allowed = (key_at <= query_at) & (key_at >= twice(begin_row))

        def body(n, _):
            offset = (kv * 4 + n) * 2 * TOKENS
            part = lanes(offset, 2 * TOKENS)
            q_two = q[:, part]
            do_two = do[:, part]
            query = jnp.concatenate([q_two[:, :TOKENS], q_two[:, TOKENS:]], axis=0)
            cotangent = jnp.concatenate([do_two[:, :TOKENS], do_two[:, TOKENS:]], axis=0)
            score = jnp.where(allowed, nt(key, query) * SCALE, MASKED)
            top = jnp.max(score, axis=0, keepdims=True)
            weight = jnp.exp(score - top)
            total = jnp.sum(weight, axis=0, keepdims=True)
            prob = weight * (1.0 / total)
            reply = nt(value, cotangent)
            centre = jnp.sum(prob * reply, axis=0, keepdims=True)
            score_grad = (prob * (reply - centre)).astype(BF16)
            query_grad = (tn(score_grad, key) * SCALE).astype(BF16)
            gq[:, part] = jnp.concatenate([query_grad[:TOKENS], query_grad[TOKENS:]], axis=1)
            dacc[kv, :, 0:TOKENS] += nn(score_grad, query) * SCALE
            dacc[kv, :, TOKENS : 2 * TOKENS] += nn(prob.astype(BF16), cotangent)
            return 0

        lax.fori_loop(first, last, body, 0)

    def d_copy(kv, hop):
        return remote(
            dsend.at[kv, hop], drecv.at[kv, hop], dss.at[kv, hop], drs.at[kv, hop], {"ctx": left}
        )

    def d_hop(kv, hop):
        own = dacc[kv, hop * TOKENS : (hop + 1) * TOKENS]
        if hop > 0:
            d_copy(kv, hop - 1).wait_recv()
            own = own + drecv[kv, hop - 1].astype(F32)
        if hop < REACH:
            dsend[kv, hop] = own.astype(BF16)
            d_copy(kv, hop).start()
        else:
            gk[:, kv * TOKENS : (kv + 1) * TOKENS] = own[:, :TOKENS].astype(BF16)
            gv[:, kv * TOKENS : (kv + 1) * TOKENS] = own[:, TOKENS:].astype(BF16)

    def gating(part):
        g_here = gate[:, part].astype(F32)
        sigma = jax.nn.sigmoid(g_here)
        activation = g_here * sigma
        out_grad = dout[:, part].astype(F32)
        return g_here, sigma, activation, out_grad, out_grad * gain[0:1, part]

    def middle(ch, g):
        part = lanes(ch * CHUNK, CHUNK)
        entered = nn(group(c, g), frecv[1, ch]) * sve[:, part]
        carried[:, part] = entered.astype(BF16)
        here = mixed[:, part] + entered
        mixed[:, part] = here
        _, _, activation, _, scaled = gating(part)
        gated = here * activation
        tsum[0] += folded(gated * gated)
        tsum[1] += folded(gated * scaled)

    def f_leg_b(stage):
        for g in range(groups):
            leg_b(f_copy, fsend, frecv, loc, f_chunk(stage, g), stage)

    def f_middle(stage):
        for g in range(groups):
            middle(f_chunk(stage, g), g)

    tsum[...] = jnp.zeros_like(tsum)
    dacc[...] = jnp.zeros_like(dacc)
    dgram[...] = jnp.zeros_like(dgram)
    dc[...] = jnp.zeros_like(dc)
    db[...] = jnp.zeros_like(db)
    hsum[...] = jnp.zeros_like(hsum)

    def gather_window():
        for kv in range(KV):
            head = slice(kv * TOKENS, (kv + 1) * TOKENS)
            for slot in range(REACH + 1):
                window = slice(slot * TOKENS, (slot + 1) * TOKENS)
                kall[kv, window] = kw[slot, :, head] if slot < REACH else k[:, head]
                vall[kv, window] = vw[slot, :, head] if slot < REACH else v[:, head]

    stores = [
        pltpu.make_async_copy(result, output, outs.at[n])
        for n, (result, output) in enumerate(((ggate, ggate_out), (gq, gq_out), (gx, gx_out)))
    ]

    f_leg_a(1)
    inside_pair(0, 0, 8)
    f_leg_a(2)
    inside_pair(1, 0, 8)
    f_leg_a(3)
    kv_wait(0)
    kv_start(1)
    loaded(gate, dout, q, do)
    f_leg_b(0)
    f_middle(0)
    f_leg_b(1)
    f_middle(1)
    f_leg_b(2)
    f_middle(2)
    f_leg_b(3)
    kv_wait(1)
    kv_start(2)
    f_middle(3)

    ones = jnp.ones((8, TOKENS), F32)
    squares = nt(ones, tsum[0], HIGH)
    crosses = nt(ones, tsum[1], HIGH)
    message = jnp.where(iota((8, TOKENS), 0) == 0, squares, crosses)
    tmsg[...] = message
    tbuf[tp] = message

    def t_copy(peer, slot):
        return remote(tmsg, tbuf.at[slot], tss.at[peer], trs.at[slot], {"tp": peer})

    for peer in tp_peers:
        t_copy(peer, tp).start()
    for peer in tp_peers:
        t_copy(peer, peer).wait_recv()
    total = tbuf[0] + tbuf[1] + tbuf[2] + tbuf[3]
    factor = lax.rsqrt(total[0:1] / NORM_WIDTH + EPSILON)
    pull = factor * factor * factor * total[1:2] / NORM_WIDTH
    cols[0] = turned(factor)
    cols[1] = turned(pull)

    def cotangents(ch, g):
        part = lanes(ch * CHUNK, CHUNK)
        g_here, sigma, activation, out_grad, scaled = gating(part)
        here = mixed[:, part]
        gated = here * activation
        factor_col = twice(cols[0])
        gated_grad = factor_col * scaled - gated * twice(cols[1])
        mixed_grad = gated_grad * activation
        dy[:, part] = mixed_grad.astype(BF16)
        dsl[ch] = tn(group(c, g), (mixed_grad * sve[:, part]).astype(BF16))
        gate_grad = gated_grad * here * sigma * (1.0 + g_here * (1.0 - sigma))
        ggate[:, part] = gate_grad.astype(BF16)
        rows[2:3, part] = jnp.sum(out_grad * gated * factor_col, axis=0, keepdims=True)

    def side_sums(ch, g):
        part = lanes(ch * CHUNK, CHUNK)
        mixed_grad = dy[:, part].astype(F32)
        mark_part = marks[:, part]
        dc[g] += nt((mixed_grad * sve[:, part]).astype(BF16), frecv[1, ch])
        hsum[0] += nt(mark_part, (mixed_grad * carried[:, part].astype(F32)).astype(BF16))
        hsum[1] += nt(mark_part, (mixed_grad * x[:, part].astype(F32)).astype(BF16))

    for g in range(groups):
        cotangents(b_chunk(0, g), g)
    b_leg_a(0)
    for stage in range(1, 4):
        for g in range(groups):
            cotangents(b_chunk(stage, g), g)

    before = (row_id < lane_id).astype(BF16)
    not_before = row_id >= lane_id

    def inside_back(g, first, last):
        def body(n, _):
            pair = g * pairs + n
            part = lanes(pair * TOKENS, TOKENS)
            dy_part = dy[:, part]
            zero = jnp.zeros_like(dy_part)
            split = jnp.concatenate(
                [jnp.where(left_half, dy_part, zero), jnp.where(left_half, zero, dy_part)], axis=0
            )
            weight_grad = nt(split, x[:, part])
            w_two = w[pl.ds(pair * 2, 2)].reshape(2 * TOKENS, TOKENS)
            ls_two = ls[pl.ds(pair * 2, 2)].reshape(2 * TOKENS, TOKENS)
            spread = weight_grad * ls_two.astype(F32)
            dgram[g] += spread[:TOKENS] + spread[TOKENS:]
            moment = weight_grad * w_two.astype(F32)
            crossing = nn(moment.astype(BF16), before)
            for e in range(2):
                half = slice(e * TOKENS, (e + 1) * TOKENS)
                row = pl.ds(pair * 2 + e, 1)
                heads[3, row, :] = jnp.sum(moment[half], axis=0, keepdims=True)
                heads[4, row, :] = jnp.sum(
                    jnp.where(not_before, crossing[half], 0.0), axis=0, keepdims=True
                )
            dxin[:, part] = tn(w_two, split)
            return 0

        lax.fori_loop(first, last, body, 0)

    def tail_rates(ch, g):
        part = lanes(ch * CHUNK, CHUNK)
        later = brecv[1, ch]
        mark_part = marks[:, part]
        scaled_grad = nn(group(b, g), later)
        hsum[2] += nt(mark_part, (x[:, part].astype(F32) * scaled_grad).astype(BF16))
        hsum[3] += nt(mark_part, (later.astype(F32) * frecv[1, ch].astype(F32)).astype(BF16))
        dxin[:, part] += rows[1:2, part] * dy[:, part].astype(F32) + scaled_grad * tse[:, part]

    def finish(ch, g):
        part = lanes(ch * CHUNK, CHUNK)
        gx[:, part] = dxin[:, part].astype(BF16)
        db[g] += nt((x[:, part].astype(F32) * tse[:, part]).astype(BF16), brecv[1, ch])

    def b_leg_b(stage):
        for g in range(groups):
            leg_b(b_copy, bsend, brecv, dsl, b_chunk(stage, g), stage)

    def at_stage(work, stage):
        for g in range(groups):
            work(b_chunk(stage, g), g)

    pieces = channels // TOKENS
    z_refs = ((zmsg, zbuf), (zlate, zlbuf))
    x_refs = ((xmsg, xbuf), (xlate, xlbuf))

    def padded(a):
        return jnp.concatenate([a, jnp.zeros((TOKENS - a.shape[0], TOKENS), F32)], axis=0)

    def z_copy(turn, n, slot):
        message, slots = z_refs[turn]
        return remote(
            message, slots.at[slot], zss.at[turn, n], zrs.at[turn, slot], {"ctx": z_peers[n]}
        )

    def x_copy(turn, n, slot):
        message, slots = x_refs[turn]
        return remote(message, slots.at[slot], xss.at[turn, n], xrs.at[turn, slot], xc_ids[n])

    def z_start(turn):
        message, slots = z_refs[turn]
        slots[z] = message[...]
        for n in range(Z_SIZE - 1):
            z_copy(turn, n, z).start()

    def x_start(turn):
        slots = z_refs[turn][1]
        for n in range(Z_SIZE - 1):
            z_copy(turn, n, lax.rem(z + n + 1, Z_SIZE)).wait_recv()
        total = slots[0]
        for n in range(1, Z_SIZE):
            total = total + slots[n]
        message, slots = x_refs[turn]
        message[...] = total
        slots[xc] = total
        for n in range(X_SIZE * CORES - 1):
            x_copy(turn, n, xc).start()

    def x_total(turn):
        slots = x_refs[turn][1]
        for n in range(X_SIZE * CORES - 1):
            x_copy(turn, n, xc_peers[n]).wait_recv()
        total = slots[0]
        for n in range(1, X_SIZE * CORES):
            total = total + slots[n]
        return total

    def early_sums():
        for n in range(pieces):
            zmsg[n : n + 1] = rows[2:3, n * TOKENS : (n + 1) * TOKENS]
        zmsg[pieces : pieces + 8] = nt(ones, padded(hsum[1]), HIGH)
        z_start(0)

    stores[0].start()
    kv_wait(2)
    kv_start(3)
    inside_back(0, 0, pairs)
    b_leg_a(1)
    kv_wait(3)
    gather_window()
    attention(0, 0, 2)
    b_leg_a(2)
    attention(0, 2, 4)
    b_leg_a(3)
    d_hop(0, 0)
    attention(1, 0, 2)
    b_leg_b(0)
    d_hop(0, 1)
    attention(1, 2, 4)
    stores[1].start()
    b_leg_b(1)
    d_hop(1, 0)
    inside_back(1, 0, pairs)
    d_hop(0, 2)
    b_leg_b(2)
    for stage in range(3):
        at_stage(tail_rates, stage)
    for stage in range(4):
        at_stage(side_sums, stage)
    early_sums()
    heads[5] = nn(hsum[0], not_before.astype(F32), HIGH) + heads[4]
    d_hop(1, 1)
    d_hop(0, 3)
    b_leg_b(3)
    at_stage(tail_rates, 3)

    step = heads[0]
    tail = heads[2]
    rate = jnp.exp(column(rate_log[...]))
    tail_sum = hsum[2]
    over = jnp.sum(hsum[3], axis=1, keepdims=True)
    cum_end = heads[1][:, TOKENS - 1 :]
    whole = jnp.where(begin_last < 0, jnp.exp(cum_end), 0.0)
    decay = -rate * step
    spilled = tail * step * tail_sum
    rate_part = decay * (heads[5] + whole * over) + spilled * (cum_end - heads[1])
    zlate[...] = nt(ones, padded(rate_part), HIGH)
    z_start(1)
    d_hop(1, 2)
    for stage in range(4):
        at_stage(finish, stage)
    stores[2].start()
    d_hop(0, 4)
    x_start(0)
    d_hop(1, 3)

    log_grad = heads[5] + whole * over + nn(spilled, before.astype(F32), HIGH)
    step_grad = heads[3] / step + tail * tail_sum - rate * log_grad
    shifted = raw[...] + column(bias[...])
    graw[...] = jax.nn.sigmoid(shifted) * step_grad
    for g in range(groups):
        spread = dgram[g].astype(BF16)
        part = slice(g * TOKENS, (g + 1) * TOKENS)
        gc[:, part] = (dc[g] + nn(spread, group(b, g))).astype(BF16)
        gb[:, part] = (db[g] + tn(spread, group(c, g))).astype(BF16)

    x_start(1)
    d_hop(1, 4)
    total = x_total(0)
    for n in range(pieces):
        ggain[0:1, n * TOKENS : (n + 1) * TOKENS] = total[n : n + 1]
    gskip[...] = total[pieces : pieces + 1, :n_heads]
    total = x_total(1)
    grate[...] = total[0:1, :n_heads]

    for store in stores:
        store.wait()
    for hop in range(REACH):
        for copy in kv_copies(hop):
            copy.wait_send()
        for kv in range(KV):
            d_copy(kv, hop).wait_send()
    for copy, chunk in ((f_copy, f_chunk), (b_copy, b_chunk)):
        for stage in range(4):
            for g in range(groups):
                ch = chunk(stage, g)
                for n in range(TOKENS // CUT):
                    copy(0, ch, 0, n).wait_send()
                    if stage < 3:
                        copy(1, ch, 1, n).wait_send()
    for peer in tp_peers:
        t_copy(peer, tp).wait_send()
    for turn in range(2):
        for n in range(Z_SIZE - 1):
            z_copy(turn, n, z).wait_send()
        for n in range(X_SIZE * CORES - 1):
            x_copy(turn, n, xc).wait_send()


def hand_over(*refs):
    results, outputs, held, arrived, left = refs[:11], refs[11:22], refs[22:33], refs[33], refs[34]
    copies = [
        (
            pltpu.make_async_copy(result, slot, arrived.at[n]),
            pltpu.make_async_copy(slot, output, left.at[n]),
        )
        for n, (result, slot, output) in enumerate(zip(results, held, outputs))
    ]
    for first, _ in copies:
        first.start()
    for first, second in copies:
        first.wait()
        second.start()
    for _, second in copies:
        second.wait()


def per_device(
    ssm_input, ssm_gate, step_raw, b_proj, c_proj, rate_log, step_bias, skip_gain, norm_gain,
    ssm_grad_out, queries, keys, values, attention_output_gradient, doc_lengths,
):
    channels = ssm_input.shape[2]
    n_heads = rate_log.shape[0]
    groups = b_proj.shape[2] // TOKENS
    chunks = channels // CHUNK
    vmem = pl.BlockSpec(memory_space=pltpu.VMEM)
    hbm = pl.BlockSpec(memory_space=pltpu.HBM)
    anywhere = pl.BlockSpec(memory_space=pl.ANY)
    smem = pl.BlockSpec(memory_space=pltpu.SMEM)
    wide = jax.ShapeDtypeStruct((TOKENS, channels), BF16)
    narrow = jax.ShapeDtypeStruct((TOKENS, groups * TOKENS), BF16)
    head_row = jax.ShapeDtypeStruct((1, n_heads), F32)
    square = (TOKENS, TOKENS)
    chunked = (chunks, TOKENS, CHUNK)
    window = (REACH + 1) * TOKENS
    message = (channels // TOKENS + 8, TOKENS)
    dma = pltpu.SemaphoreType.DMA
    scratch = [
        pltpu.VMEM((n_heads,) + square, BF16),
        pltpu.VMEM((n_heads,) + square, BF16),
        pltpu.VMEM((TOKENS, channels), F32),
        pltpu.VMEM((TOKENS, channels), BF16),
        pltpu.VMEM((TOKENS, channels), BF16),
        pltpu.VMEM((TOKENS, channels), F32),
        pltpu.VMEM((TOKENS, channels), F32),
        pltpu.VMEM((TOKENS, channels), F32),
        pltpu.VMEM((8, channels), F32),
        pltpu.VMEM((n_heads, channels), BF16),
        pltpu.VMEM((6, n_heads, TOKENS), F32),
        pltpu.VMEM((groups,) + square, F32),
        pltpu.VMEM((groups,) + square, F32),
        pltpu.VMEM(chunked, F32),
        pltpu.VMEM(chunked, F32),
        pltpu.VMEM((2,) + chunked, BF16),
        pltpu.VMEM((2,) + chunked, BF16),
        pltpu.VMEM((2,) + chunked, BF16),
        pltpu.VMEM((2,) + chunked, BF16),
        pltpu.VMEM((REACH, TOKENS, KV * TOKENS), BF16),
        pltpu.VMEM((REACH, TOKENS, KV * TOKENS), BF16),
        pltpu.VMEM((KV, window, TOKENS), BF16),
        pltpu.VMEM((KV, window, TOKENS), BF16),
        pltpu.VMEM((KV, window, 2 * TOKENS), F32),
        pltpu.VMEM((KV, REACH, TOKENS, 2 * TOKENS), BF16),
        pltpu.VMEM((KV, REACH, TOKENS, 2 * TOKENS), BF16),
        pltpu.VMEM((2,) + square, F32),
        pltpu.VMEM((8, TOKENS), F32),
        pltpu.VMEM((TP_SIZE, 8, TOKENS), F32),
        pltpu.VMEM((2,) + square, F32),
        pltpu.VMEM((groups,) + square, F32),
        pltpu.VMEM((groups,) + square, F32),
        pltpu.VMEM((4, n_heads, TOKENS), F32),
        pltpu.VMEM(message, F32),
        pltpu.VMEM((Z_SIZE,) + message, F32),
        pltpu.VMEM(message, F32),
        pltpu.VMEM((X_SIZE * CORES,) + message, F32),
        pltpu.VMEM((8, TOKENS), F32),
        pltpu.VMEM((Z_SIZE, 8, TOKENS), F32),
        pltpu.VMEM((8, TOKENS), F32),
        pltpu.VMEM((X_SIZE * CORES, 8, TOKENS), F32),
        pltpu.VMEM(wide.shape, BF16),
        pltpu.VMEM(wide.shape, BF16),
        pltpu.VMEM((n_heads, TOKENS), F32),
        pltpu.VMEM(narrow.shape, BF16),
        pltpu.VMEM(narrow.shape, BF16),
        pltpu.VMEM(wide.shape, BF16),
        pltpu.VMEM(wide.shape, BF16),
        pltpu.VMEM(narrow.shape, BF16),
        pltpu.VMEM(narrow.shape, BF16),
        pltpu.VMEM(wide.shape, BF16),
        pltpu.VMEM(wide.shape, BF16),
        pltpu.VMEM(wide.shape, BF16),
        pltpu.VMEM(wide.shape, BF16),
        dma((2, chunks, TOKENS // CUT)),
        dma((2, chunks, TOKENS // CUT)),
        dma((2, chunks, TOKENS // CUT)),
        dma((2, chunks, TOKENS // CUT)),
        dma((2, REACH)),
        dma((2, REACH)),
        dma((KV, REACH)),
        dma((KV, REACH)),
        dma((TP_SIZE,)),
        dma((TP_SIZE,)),
        dma((2, Z_SIZE)),
        dma((2, Z_SIZE)),
        dma((2, X_SIZE * CORES)),
        dma((2, X_SIZE * CORES)),
        dma((10,)),
        dma((3,)),
    ]
    shapes = (
        wide, wide, jax.ShapeDtypeStruct((n_heads, TOKENS), F32), narrow, narrow, head_row,
        head_row, jax.ShapeDtypeStruct((1, channels), F32), wide, narrow, narrow,
    )
    results = pl.pallas_call(
        kernel,
        out_shape=shapes,
        in_specs=[smem] + [hbm] * 5 + [vmem] * 4 + [hbm] * 5,
        out_specs=(hbm, hbm) + (vmem,) * 6 + (hbm, vmem, vmem),
        scratch_shapes=scratch,
        compiler_params=pltpu.CompilerParams(
            collective_id=0, has_side_effects=True, vmem_limit_bytes=VMEM_LIMIT
        ),
        name="mixer_and_attention",
    )(
        doc_lengths,
        ssm_input[0],
        ssm_gate[0],
        step_raw[0],
        b_proj[0],
        c_proj[0],
        rate_log[None],
        step_bias[None],
        skip_gain[None],
        norm_gain[None],
        ssm_grad_out[0],
        queries[0],
        keys[0],
        values[0],
        attention_output_gradient[0],
    )
    results = pl.pallas_call(
        hand_over,
        out_shape=shapes,
        in_specs=[anywhere] * 11,
        out_specs=(anywhere,) * 11,
        scratch_shapes=[pltpu.VMEM(a.shape, a.dtype) for a in shapes] + [dma((11,)), dma((11,))],
        compiler_params=pltpu.CompilerParams(vmem_limit_bytes=VMEM_LIMIT),
        name="hand_over",
    )(*results)
    gx, ggate, graw, gb, gc, grate, gskip, ggain, gq, gk, gv = results
    return (
        gx[None], ggate[None], graw[None], gb[None], gc[None],
        grate[0], gskip[0], ggain[0], gq[None], gk[None], gv[None],
    )


def solution(mesh):
    tokens = P("dp", "ctx", "tp")
    steps = P("dp", "tp", "ctx")
    param = P("tp")
    return jax.shard_map(
        per_device,
        mesh=mesh,
        in_specs=(
            tokens, tokens, steps, tokens, tokens, param, param, param, param,
            tokens, tokens, tokens, tokens, tokens, P("dp", None),
        ),
        out_specs=(
            tokens, tokens, steps, tokens, tokens, param, param, param,
            tokens, tokens, tokens,
        ),
        check_vma=False,
    )
```

```python
import jax
import jax.numpy as jnp
from jax import lax
from jax.experimental import pallas as pl
from jax.experimental.pallas import tpu as pltpu
from jax.sharding import PartitionSpec as P

MESH = pl.DeviceIdType.MESH
F32 = jnp.float32
BF16 = jnp.bfloat16
HIGH = lax.Precision.HIGHEST

TOKENS = 128
WIDE = 64
REACH = 4
CHUNK = 256
CUT = 64
KV = 2
NORM_WIDTH = 8192
EPSILON = 1e-05
MASKED = -1e30
SCALE = 128.0**-0.5
Z_SIZE = 8
X_SIZE = 4
CORES = 2
VMEM_LIMIT = 62000000
TP_SIZE = 4


def dot(a, b, dims, precision=None):
    return lax.dot_general(
        a, b, (dims, ((), ())), precision=precision, preferred_element_type=F32
    )


def nn(a, b, precision=None):
    return dot(a, b, ((1,), (0,)), precision)


def nt(a, b, precision=None):
    return dot(a, b, ((1,), (1,)), precision)


def tn(a, b, precision=None):
    return dot(a, b, ((0,), (0,)), precision)


def iota(shape, axis):
    return lax.broadcasted_iota(jnp.int32, shape, axis)


def lanes(start, size):
    return pl.ds(pl.multiple_of(start, size), size)


def column(row):
    size = row.shape[1]
    on_diagonal = iota((size, size), 0) == iota((size, size), 1)
    return jnp.sum(jnp.where(on_diagonal, row, 0.0), axis=1, keepdims=True)


def turned(row):
    return jnp.transpose(jnp.broadcast_to(row, (TOKENS, TOKENS)))


def twice(a):
    return jnp.concatenate([a, a], axis=1)


def folded(a):
    return a[:, :TOKENS] + a[:, TOKENS:]


def kernel(
    lens, x_in, gate_in, raw_in, b_in, c_in, rate_log, bias, skip, gain,
    dout_in, q_in, k_in, v_in, do_in,
    gx_out, ggate_out, graw, gb, gc, grate, gskip, ggain, gq_out, gk, gv,
    ls, w, mixed, carried, dy, dxin, sve, tse, rows, marks, heads,
    gram, dgram, loc, dsl, fsend, frecv, bsend, brecv, kw, vw, kall, vall,
    dacc, dsend, drecv, tsum, tmsg, tbuf, cols, dc, db, hsum, zmsg, zbuf, xmsg, xbuf,
    zlate, zlbuf, xlate, xlbuf, x, gate, raw, b, c, dout, q, k, v, do,
    gx, ggate, gq, fss, frs, bss, brs, kss, krs, dss, drs, tss, trs, zss, zrs, xss, xrs, ins, outs,
):
    i = lax.axis_index("ctx")
    core = lax.axis_index("dp")
    tp = lax.axis_index("tp")
    count = Z_SIZE * X_SIZE
    right = lax.rem(i + 1, count)
    left = lax.rem(i + count - 1, count)
    z = lax.rem(i, Z_SIZE)
    xi = i // Z_SIZE
    xc = xi * CORES + core
    z_peers = [xi * Z_SIZE + lax.rem(z + n, Z_SIZE) for n in range(1, Z_SIZE)]
    xc_peers = [lax.rem(xc + n, X_SIZE * CORES) for n in range(1, X_SIZE * CORES)]
    xc_ids = [{"ctx": (p // CORES) * Z_SIZE + z, "dp": lax.rem(p, CORES)} for p in xc_peers]
    tp_peers = [lax.rem(tp + n, TP_SIZE) for n in range(1, TP_SIZE)]
    n_heads = raw.shape[0]
    channels = x.shape[1]
    groups = b.shape[1] // TOKENS
    pairs = n_heads // 2 // groups

    barrier = pltpu.get_barrier_semaphore()
    greeted = (
        [{"ctx": left}, {"ctx": right}]
        + [{"tp": p} for p in tp_peers]
        + [{"ctx": p} for p in z_peers]
        + xc_ids
    )
    for device in greeted:
        pl.semaphore_signal(barrier, inc=1, device_id=device, device_id_type=MESH)

    loads = []
    for source, target in (
        (raw_in, raw), (x_in, x), (b_in, b), (c_in, c), (k_in, k), (v_in, v),
        (gate_in, gate), (dout_in, dout), (q_in, q), (do_in, do),
    ):
        loads.append((target, pltpu.make_async_copy(source, target, ins.at[len(loads)])))
        loads[-1][1].start()

    def loaded(*targets):
        for target, load in loads:
            if any(target is wanted for wanted in targets):
                load.wait()

    def remote(source, target, send, recv, device):
        return pltpu.make_async_remote_copy(
            src_ref=source,
            dst_ref=target,
            send_sem=send,
            recv_sem=recv,
            device_id=device,
            device_id_type=MESH,
        )

    def kv_copies(hop):
        slot = REACH - 1 - hop
        k_from = k if hop == 0 else kw.at[slot + 1]
        v_from = v if hop == 0 else vw.at[slot + 1]
        to = {"ctx": right}
        return (
            remote(k_from, kw.at[slot], kss.at[0, hop], krs.at[0, hop], to),
            remote(v_from, vw.at[slot], kss.at[1, hop], krs.at[1, hop], to),
        )

    def kv_start(hop):
        for copy in kv_copies(hop):
            copy.start()

    def kv_wait(hop):
        for copy in kv_copies(hop):
            copy.wait_recv()

    base = i * TOKENS
    position = iota((8, TOKENS), 1) + base
    begin = jnp.zeros((8, TOKENS), jnp.int32)
    end = jnp.int32(0)
    for d in range(lens.shape[1]):
        end = end + lens[0, d]
        begin = begin + jnp.where(position >= end, lens[0, d], 0)
    begin_row = (begin - base)[0:1]
    begin_last = begin_row[:, TOKENS - 1 :]
    begin_col = turned(begin_row.astype(F32))
    row_id = iota((TOKENS, TOKENS), 0)
    lane_id = iota((TOKENS, TOKENS), 1)
    within = (lane_id <= row_id) & (lane_id.astype(F32) >= begin_col)
    up_to = (row_id <= lane_id).astype(F32)

    loaded(raw)
    shifted = raw[...] + column(bias[...])
    step = jax.nn.softplus(shifted)
    rate = jnp.exp(column(rate_log[...]))
    decay = -rate * step
    cum = nn(decay, up_to, HIGH)
    cum_end = cum[:, TOKENS - 1 :]
    survive = jnp.where(begin_row < 0, jnp.exp(cum), 0.0)
    tail = jnp.where(iota((1, TOKENS), 1) >= begin_last, jnp.exp(cum_end - cum), 0.0)
    whole = jnp.where(begin_last < 0, jnp.exp(cum_end), 0.0)
    heads[0] = step
    heads[1] = cum
    heads[2] = tail
    mark = iota((n_heads, channels), 1) // WIDE == iota((n_heads, channels), 0)
    marks[...] = mark.astype(BF16)
    both = jnp.concatenate([marks[...], marks[...]], axis=0)

    def expand(a):
        high = a.astype(BF16)
        low = (a - high.astype(F32)).astype(BF16)
        return tn(jnp.concatenate([high, low], axis=0), both)

    tse[...] = expand(tail * step)
    rows[0:1] = jnp.sum(jnp.where(mark, whole, 0.0), axis=0, keepdims=True)

    def group(a, g):
        return a[:, g * TOKENS : (g + 1) * TOKENS]

    def local_state(ch, g):
        part = lanes(ch * CHUNK, CHUNK)
        inputs = (x[:, part].astype(F32) * tse[:, part]).astype(BF16)
        loc[ch] = tn(group(b, g), inputs)

    def f_chunk(stage, g):
        return g * 4 + lax.rem(stage + 4 * count - i, 4)

    def b_chunk(stage, g):
        return g * 4 + lax.rem(stage + i, 4)

    def chain(send, recv, ss, rs, device):
        def copy(leg, ch, to, n):
            cut = slice(n * CUT, (n + 1) * CUT)
            return remote(
                send.at[leg, ch, cut], recv.at[to, ch, cut],
                ss.at[leg, ch, n], rs.at[to, ch, n], device,
            )

        return copy

    f_copy = chain(fsend, frecv, fss, frs, {"ctx": right})
    b_copy = chain(bsend, brecv, bss, brs, {"ctx": left})

    def leg_a(copy, send, recv, own, ch, stage):
        for n in range(TOKENS // CUT):
            cut = slice(n * CUT, (n + 1) * CUT)
            value = own[ch, cut]
            if stage > 0:
                copy(0, ch, 0, n).wait_recv()
                decayed = rows[0:1, lanes(ch * CHUNK, CHUNK)] * recv[0, ch, cut].astype(F32)
                value = value + decayed
            send[0, ch, cut] = value.astype(BF16)
            copy(0, ch, 1 if stage == 3 else 0, n).start()

    def leg_b(copy, send, recv, own, ch, stage):
        for n in range(TOKENS // CUT):
            cut = slice(n * CUT, (n + 1) * CUT)
            copy(1, ch, 1, n).wait_recv()
            if stage < 3:
                decayed = rows[0:1, lanes(ch * CHUNK, CHUNK)] * recv[1, ch, cut].astype(F32)
                send[1, ch, cut] = (own[ch, cut] + decayed).astype(BF16)
                copy(1, ch, 1, n).start()

    def f_leg_a(stage):
        for g in range(groups):
            leg_a(f_copy, fsend, frecv, loc, f_chunk(stage, g), stage)

    def b_leg_a(stage):
        for g in range(groups):
            leg_a(b_copy, bsend, brecv, dsl, b_chunk(stage, g), stage)

    loaded(x, b)
    for g in range(groups):
        local_state(f_chunk(0, g), g)
    pl.semaphore_wait(barrier, len(greeted))
    f_leg_a(0)
    loaded(k, v)
    kv_start(0)
    for stage in range(1, 4):
        for g in range(groups):
            local_state(f_chunk(stage, g), g)
    sve[...] = expand(survive)
    rows[1:2] = jnp.sum(jnp.where(mark, column(skip[...]), 0.0), axis=0, keepdims=True)
    loaded(c)
    for g in range(groups):
        gram[g] = nt(group(c, g), group(b, g))

    left_half = iota((1, TOKENS), 1) < WIDE

    def inside_pair(g, first, last):
        def body(n, _):
            pair = g * pairs + n
            part = lanes(pair * TOKENS, TOKENS)
            for e in range(2):
                h = pair * 2 + e
                cum_row = heads[1, pl.ds(h, 1), :]
                gap = jnp.where(within, turned(cum_row) - cum_row, MASKED)
                scaled = jnp.exp(gap) * heads[0, pl.ds(h, 1), :]
                ls[h] = scaled.astype(BF16)
                w[h] = (scaled * gram[g]).astype(BF16)
            x_part = x[:, part]
            product = nn(w[pl.ds(pair * 2, 2)].reshape(2 * TOKENS, TOKENS), x_part)
            inside = jnp.where(left_half, product[:TOKENS], product[TOKENS:])
            mixed[:, part] = inside + rows[1:2, part] * x_part.astype(F32)
            return 0

        lax.fori_loop(first, last, body, 0)

    def attention(kv, first, last):
        key = kall[kv]
        value = vall[kv]
        window = (REACH + 1) * TOKENS
        key_at = iota((window, 2 * TOKENS), 0) - REACH * TOKENS
        query_at = twice(iota((1, TOKENS), 1))
        allowed = (key_at <= query_at) & (key_at >= twice(begin_row))

        def body(n, _):
            offset = (kv * 4 + n) * 2 * TOKENS
            part = lanes(offset, 2 * TOKENS)
            q_two = q[:, part]
            do_two = do[:, part]
            query = jnp.concatenate([q_two[:, :TOKENS], q_two[:, TOKENS:]], axis=0)
            cotangent = jnp.concatenate([do_two[:, :TOKENS], do_two[:, TOKENS:]], axis=0)
            score = jnp.where(allowed, nt(key, query) * SCALE, MASKED)
            top = jnp.max(score, axis=0, keepdims=True)
            weight = jnp.exp(score - top)
            total = jnp.sum(weight, axis=0, keepdims=True)
            prob = weight * (1.0 / total)
            reply = nt(value, cotangent)
            centre = jnp.sum(prob * reply, axis=0, keepdims=True)
            score_grad = (prob * (reply - centre)).astype(BF16)
            query_grad = (tn(score_grad, key) * SCALE).astype(BF16)
            gq[:, part] = jnp.concatenate([query_grad[:TOKENS], query_grad[TOKENS:]], axis=1)
            dacc[kv, :, 0:TOKENS] += nn(score_grad, query) * SCALE
            dacc[kv, :, TOKENS : 2 * TOKENS] += nn(prob.astype(BF16), cotangent)
            return 0

        lax.fori_loop(first, last, body, 0)

    def d_copy(kv, hop):
        return remote(
            dsend.at[kv, hop], drecv.at[kv, hop], dss.at[kv, hop], drs.at[kv, hop], {"ctx": left}
        )

    def d_hop(kv, hop):
        own = dacc[kv, hop * TOKENS : (hop + 1) * TOKENS]
        if hop > 0:
            d_copy(kv, hop - 1).wait_recv()
            own = own + drecv[kv, hop - 1].astype(F32)
        if hop < REACH:
            dsend[kv, hop] = own.astype(BF16)
            d_copy(kv, hop).start()
        else:
            gk[:, kv * TOKENS : (kv + 1) * TOKENS] = own[:, :TOKENS].astype(BF16)
            gv[:, kv * TOKENS : (kv + 1) * TOKENS] = own[:, TOKENS:].astype(BF16)

    def gating(part):
        g_here = gate[:, part].astype(F32)
        sigma = jax.nn.sigmoid(g_here)
        activation = g_here * sigma
        out_grad = dout[:, part].astype(F32)
        return g_here, sigma, activation, out_grad, out_grad * gain[0:1, part]

    def middle(ch, g):
        part = lanes(ch * CHUNK, CHUNK)
        entered = nn(group(c, g), frecv[1, ch]) * sve[:, part]
        carried[:, part] = entered.astype(BF16)
        here = mixed[:, part] + entered
        mixed[:, part] = here
        _, _, activation, _, scaled = gating(part)
        gated = here * activation
        tsum[0] += folded(gated * gated)
        tsum[1] += folded(gated * scaled)

    def f_leg_b(stage):
        for g in range(groups):
            leg_b(f_copy, fsend, frecv, loc, f_chunk(stage, g), stage)

    def f_middle(stage):
        for g in range(groups):
            middle(f_chunk(stage, g), g)

    tsum[...] = jnp.zeros_like(tsum)
    dacc[...] = jnp.zeros_like(dacc)
    dgram[...] = jnp.zeros_like(dgram)
    dc[...] = jnp.zeros_like(dc)
    db[...] = jnp.zeros_like(db)
    hsum[...] = jnp.zeros_like(hsum)

    def gather_window():
        for kv in range(KV):
            head = slice(kv * TOKENS, (kv + 1) * TOKENS)
            for slot in range(REACH + 1):
                window = slice(slot * TOKENS, (slot + 1) * TOKENS)
                kall[kv, window] = kw[slot, :, head] if slot < REACH else k[:, head]
                vall[kv, window] = vw[slot, :, head] if slot < REACH else v[:, head]

    stores = [
        pltpu.make_async_copy(result, output, outs.at[n])
        for n, (result, output) in enumerate(((ggate, ggate_out), (gq, gq_out), (gx, gx_out)))
    ]

    f_leg_a(1)
    inside_pair(0, 0, 8)
    f_leg_a(2)
    inside_pair(1, 0, 8)
    f_leg_a(3)
    kv_wait(0)
    kv_start(1)
    loaded(gate, dout, q, do)
    f_leg_b(0)
    f_middle(0)
    f_leg_b(1)
    f_middle(1)
    f_leg_b(2)
    f_middle(2)
    f_leg_b(3)
    kv_wait(1)
    kv_start(2)
    f_middle(3)

    ones = jnp.ones((8, TOKENS), F32)
    squares = nt(ones, tsum[0], HIGH)
    crosses = nt(ones, tsum[1], HIGH)
    message = jnp.where(iota((8, TOKENS), 0) == 0, squares, crosses)
    tmsg[...] = message
    tbuf[tp] = message

    def t_copy(peer, slot):
        return remote(tmsg, tbuf.at[slot], tss.at[peer], trs.at[slot], {"tp": peer})

    for peer in tp_peers:
        t_copy(peer, tp).start()
    for peer in tp_peers:
        t_copy(peer, peer).wait_recv()
    total = tbuf[0] + tbuf[1] + tbuf[2] + tbuf[3]
    factor = lax.rsqrt(total[0:1] / NORM_WIDTH + EPSILON)
    pull = factor * factor * factor * total[1:2] / NORM_WIDTH
    cols[0] = turned(factor)
    cols[1] = turned(pull)

    def cotangents(ch, g):
        part = lanes(ch * CHUNK, CHUNK)
        _, _, activation, _, scaled = gating(part)
        gated = mixed[:, part] * activation
        gated_grad = twice(cols[0]) * scaled - gated * twice(cols[1])
        mixed_grad = gated_grad * activation
        dy[:, part] = mixed_grad.astype(BF16)
        dsl[ch] = tn(group(c, g), (mixed_grad * sve[:, part]).astype(BF16))

    def gate_grads(ch, g):
        part = lanes(ch * CHUNK, CHUNK)
        g_here, sigma, activation, out_grad, scaled = gating(part)
        here = mixed[:, part]
        gated = here * activation
        factor_col = twice(cols[0])
        gated_grad = factor_col * scaled - gated * twice(cols[1])
        gate_grad = gated_grad * here * sigma * (1.0 + g_here * (1.0 - sigma))
        ggate[:, part] = gate_grad.astype(BF16)
        rows[2:3, part] = jnp.sum(out_grad * gated * factor_col, axis=0, keepdims=True)

    def side_sums(ch, g):
        part = lanes(ch * CHUNK, CHUNK)
        mixed_grad = dy[:, part].astype(F32)
        mark_part = marks[:, part]
        dc[g] += nt((mixed_grad * sve[:, part]).astype(BF16), frecv[1, ch])
        hsum[0] += nt(mark_part, (mixed_grad * carried[:, part].astype(F32)).astype(BF16))
        hsum[1] += nt(mark_part, (mixed_grad * x[:, part].astype(F32)).astype(BF16))

    for g in range(groups):
        cotangents(b_chunk(0, g), g)
    b_leg_a(0)
    for stage in range(1, 4):
        for g in range(groups):
            cotangents(b_chunk(stage, g), g)

    before = (row_id < lane_id).astype(BF16)
    not_before = row_id >= lane_id

    def inside_back(g, first, last):
        def body(n, _):
            pair = g * pairs + n
            part = lanes(pair * TOKENS, TOKENS)
            dy_part = dy[:, part]
            zero = jnp.zeros_like(dy_part)
            split = jnp.concatenate(
                [jnp.where(left_half, dy_part, zero), jnp.where(left_half, zero, dy_part)], axis=0
            )
            weight_grad = nt(split, x[:, part])
            w_two = w[pl.ds(pair * 2, 2)].reshape(2 * TOKENS, TOKENS)
            ls_two = ls[pl.ds(pair * 2, 2)].reshape(2 * TOKENS, TOKENS)
            spread = weight_grad * ls_two.astype(F32)
            dgram[g] += spread[:TOKENS] + spread[TOKENS:]
            moment = weight_grad * w_two.astype(F32)
            crossing = nn(moment.astype(BF16), before)
            for e in range(2):
                half = slice(e * TOKENS, (e + 1) * TOKENS)
                row = pl.ds(pair * 2 + e, 1)
                heads[3, row, :] = jnp.sum(moment[half], axis=0, keepdims=True)
                heads[4, row, :] = jnp.sum(
                    jnp.where(not_before, crossing[half], 0.0), axis=0, keepdims=True
                )
            dxin[:, part] = tn(w_two, split)
            return 0

        lax.fori_loop(first, last, body, 0)

    def tail_rates(ch, g):
        part = lanes(ch * CHUNK, CHUNK)
        later = brecv[1, ch]
        mark_part = marks[:, part]
        scaled_grad = nn(group(b, g), later)
        hsum[2] += nt(mark_part, (x[:, part].astype(F32) * scaled_grad).astype(BF16))
        hsum[3] += nt(mark_part, (later.astype(F32) * frecv[1, ch].astype(F32)).astype(BF16))
        dxin[:, part] += rows[1:2, part] * dy[:, part].astype(F32) + scaled_grad * tse[:, part]

    def finish(ch, g):
        part = lanes(ch * CHUNK, CHUNK)
        gx[:, part] = dxin[:, part].astype(BF16)
        db[g] += nt((x[:, part].astype(F32) * tse[:, part]).astype(BF16), brecv[1, ch])

    def b_leg_b(stage):
        for g in range(groups):
            leg_b(b_copy, bsend, brecv, dsl, b_chunk(stage, g), stage)

    def at_stage(work, stage):
        for g in range(groups):
            work(b_chunk(stage, g), g)

    pieces = channels // TOKENS
    z_refs = ((zmsg, zbuf), (zlate, zlbuf))
    x_refs = ((xmsg, xbuf), (xlate, xlbuf))

    def padded(a):
        return jnp.concatenate([a, jnp.zeros((TOKENS - a.shape[0], TOKENS), F32)], axis=0)

    def z_copy(turn, n, slot):
        message, slots = z_refs[turn]
        return remote(
            message, slots.at[slot], zss.at[turn, n], zrs.at[turn, slot], {"ctx": z_peers[n]}
        )

    def x_copy(turn, n, slot):
        message, slots = x_refs[turn]
        return remote(message, slots.at[slot], xss.at[turn, n], xrs.at[turn, slot], xc_ids[n])

    def z_start(turn):
        message, slots = z_refs[turn]
        slots[z] = message[...]
        for n in range(Z_SIZE - 1):
            z_copy(turn, n, z).start()

    def x_start(turn):
        slots = z_refs[turn][1]
        for n in range(Z_SIZE - 1):
            z_copy(turn, n, lax.rem(z + n + 1, Z_SIZE)).wait_recv()
        total = slots[0]
        for n in range(1, Z_SIZE):
            total = total + slots[n]
        message, slots = x_refs[turn]
        message[...] = total
        slots[xc] = total
        for n in range(X_SIZE * CORES - 1):
            x_copy(turn, n, xc).start()

    def x_total(turn):
        slots = x_refs[turn][1]
        for n in range(X_SIZE * CORES - 1):
            x_copy(turn, n, xc_peers[n]).wait_recv()
        total = slots[0]
        for n in range(1, X_SIZE * CORES):
            total = total + slots[n]
        return total

    def early_sums():
        for n in range(pieces):
            zmsg[n : n + 1] = rows[2:3, n * TOKENS : (n + 1) * TOKENS]
        zmsg[pieces : pieces + 8] = nt(ones, padded(hsum[1]), HIGH)
        z_start(0)

    for stage in range(4):
        at_stage(gate_grads, stage)
    stores[0].start()
    kv_wait(2)
    kv_start(3)
    inside_back(0, 0, pairs)
    b_leg_a(1)
    kv_wait(3)
    gather_window()
    attention(0, 0, 2)
    b_leg_a(2)
    attention(0, 2, 4)
    d_hop(0, 0)
    b_leg_a(3)
    attention(1, 0, 2)
    b_leg_b(0)
    d_hop(0, 1)
    attention(1, 2, 4)
    stores[1].start()
    d_hop(1, 0)
    b_leg_b(1)
    inside_back(1, 0, pairs)
    d_hop(0, 2)
    b_leg_b(2)
    for stage in range(3):
        at_stage(tail_rates, stage)
    for stage in range(4):
        at_stage(side_sums, stage)
    early_sums()
    heads[5] = nn(hsum[0], not_before.astype(F32), HIGH) + heads[4]
    d_hop(1, 1)
    d_hop(0, 3)
    b_leg_b(3)
    at_stage(tail_rates, 3)

    step = heads[0]
    tail = heads[2]
    rate = jnp.exp(column(rate_log[...]))
    tail_sum = hsum[2]
    over = jnp.sum(hsum[3], axis=1, keepdims=True)
    cum_end = heads[1][:, TOKENS - 1 :]
    whole = jnp.where(begin_last < 0, jnp.exp(cum_end), 0.0)
    decay = -rate * step
    spilled = tail * step * tail_sum
    rate_part = decay * (heads[5] + whole * over) + spilled * (cum_end - heads[1])
    zlate[...] = nt(ones, padded(rate_part), HIGH)
    z_start(1)
    d_hop(1, 2)
    for stage in range(4):
        at_stage(finish, stage)
    stores[2].start()
    d_hop(0, 4)
    x_start(0)
    d_hop(1, 3)

    log_grad = heads[5] + whole * over + nn(spilled, before.astype(F32), HIGH)
    step_grad = heads[3] / step + tail * tail_sum - rate * log_grad
    shifted = raw[...] + column(bias[...])
    graw[...] = jax.nn.sigmoid(shifted) * step_grad
    for g in range(groups):
        spread = dgram[g].astype(BF16)
        part = slice(g * TOKENS, (g + 1) * TOKENS)
        gc[:, part] = (dc[g] + nn(spread, group(b, g))).astype(BF16)
        gb[:, part] = (db[g] + tn(spread, group(c, g))).astype(BF16)

    x_start(1)
    d_hop(1, 4)
    total = x_total(0)
    for n in range(pieces):
        ggain[0:1, n * TOKENS : (n + 1) * TOKENS] = total[n : n + 1]
    gskip[...] = total[pieces : pieces + 1, :n_heads]
    total = x_total(1)
    grate[...] = total[0:1, :n_heads]

    for store in stores:
        store.wait()
    for hop in range(REACH):
        for copy in kv_copies(hop):
            copy.wait_send()
        for kv in range(KV):
            d_copy(kv, hop).wait_send()
    for copy, chunk in ((f_copy, f_chunk), (b_copy, b_chunk)):
        for stage in range(4):
            for g in range(groups):
                ch = chunk(stage, g)
                for n in range(TOKENS // CUT):
                    copy(0, ch, 0, n).wait_send()
                    if stage < 3:
                        copy(1, ch, 1, n).wait_send()
    for peer in tp_peers:
        t_copy(peer, tp).wait_send()
    for turn in range(2):
        for n in range(Z_SIZE - 1):
            z_copy(turn, n, z).wait_send()
        for n in range(X_SIZE * CORES - 1):
            x_copy(turn, n, xc).wait_send()


def hand_over(*refs):
    results, outputs, held, arrived, left = refs[:11], refs[11:22], refs[22:33], refs[33], refs[34]
    copies = [
        (
            pltpu.make_async_copy(result, slot, arrived.at[n]),
            pltpu.make_async_copy(slot, output, left.at[n]),
        )
        for n, (result, slot, output) in enumerate(zip(results, held, outputs))
    ]
    for first, _ in copies:
        first.start()
    for first, second in copies:
        first.wait()
        second.start()
    for _, second in copies:
        second.wait()


def per_device(
    ssm_input, ssm_gate, step_raw, b_proj, c_proj, rate_log, step_bias, skip_gain, norm_gain,
    ssm_grad_out, queries, keys, values, attention_output_gradient, doc_lengths,
):
    channels = ssm_input.shape[2]
    n_heads = rate_log.shape[0]
    groups = b_proj.shape[2] // TOKENS
    chunks = channels // CHUNK
    vmem = pl.BlockSpec(memory_space=pltpu.VMEM)
    hbm = pl.BlockSpec(memory_space=pltpu.HBM)
    anywhere = pl.BlockSpec(memory_space=pl.ANY)
    smem = pl.BlockSpec(memory_space=pltpu.SMEM)
    wide = jax.ShapeDtypeStruct((TOKENS, channels), BF16)
    narrow = jax.ShapeDtypeStruct((TOKENS, groups * TOKENS), BF16)
    head_row = jax.ShapeDtypeStruct((1, n_heads), F32)
    square = (TOKENS, TOKENS)
    chunked = (chunks, TOKENS, CHUNK)
    window = (REACH + 1) * TOKENS
    message = (channels // TOKENS + 8, TOKENS)
    dma = pltpu.SemaphoreType.DMA
    scratch = [
        pltpu.VMEM((n_heads,) + square, BF16),
        pltpu.VMEM((n_heads,) + square, BF16),
        pltpu.VMEM((TOKENS, channels), F32),
        pltpu.VMEM((TOKENS, channels), BF16),
        pltpu.VMEM((TOKENS, channels), BF16),
        pltpu.VMEM((TOKENS, channels), F32),
        pltpu.VMEM((TOKENS, channels), F32),
        pltpu.VMEM((TOKENS, channels), F32),
        pltpu.VMEM((8, channels), F32),
        pltpu.VMEM((n_heads, channels), BF16),
        pltpu.VMEM((6, n_heads, TOKENS), F32),
        pltpu.VMEM((groups,) + square, F32),
        pltpu.VMEM((groups,) + square, F32),
        pltpu.VMEM(chunked, F32),
        pltpu.VMEM(chunked, F32),
        pltpu.VMEM((2,) + chunked, BF16),
        pltpu.VMEM((2,) + chunked, BF16),
        pltpu.VMEM((2,) + chunked, BF16),
        pltpu.VMEM((2,) + chunked, BF16),
        pltpu.VMEM((REACH, TOKENS, KV * TOKENS), BF16),
        pltpu.VMEM((REACH, TOKENS, KV * TOKENS), BF16),
        pltpu.VMEM((KV, window, TOKENS), BF16),
        pltpu.VMEM((KV, window, TOKENS), BF16),
        pltpu.VMEM((KV, window, 2 * TOKENS), F32),
        pltpu.VMEM((KV, REACH, TOKENS, 2 * TOKENS), BF16),
        pltpu.VMEM((KV, REACH, TOKENS, 2 * TOKENS), BF16),
        pltpu.VMEM((2,) + square, F32),
        pltpu.VMEM((8, TOKENS), F32),
        pltpu.VMEM((TP_SIZE, 8, TOKENS), F32),
        pltpu.VMEM((2,) + square, F32),
        pltpu.VMEM((groups,) + square, F32),
        pltpu.VMEM((groups,) + square, F32),
        pltpu.VMEM((4, n_heads, TOKENS), F32),
        pltpu.VMEM(message, F32),
        pltpu.VMEM((Z_SIZE,) + message, F32),
        pltpu.VMEM(message, F32),
        pltpu.VMEM((X_SIZE * CORES,) + message, F32),
        pltpu.VMEM((8, TOKENS), F32),
        pltpu.VMEM((Z_SIZE, 8, TOKENS), F32),
        pltpu.VMEM((8, TOKENS), F32),
        pltpu.VMEM((X_SIZE * CORES, 8, TOKENS), F32),
        pltpu.VMEM(wide.shape, BF16),
        pltpu.VMEM(wide.shape, BF16),
        pltpu.VMEM((n_heads, TOKENS), F32),
        pltpu.VMEM(narrow.shape, BF16),
        pltpu.VMEM(narrow.shape, BF16),
        pltpu.VMEM(wide.shape, BF16),
        pltpu.VMEM(wide.shape, BF16),
        pltpu.VMEM(narrow.shape, BF16),
        pltpu.VMEM(narrow.shape, BF16),
        pltpu.VMEM(wide.shape, BF16),
        pltpu.VMEM(wide.shape, BF16),
        pltpu.VMEM(wide.shape, BF16),
        pltpu.VMEM(wide.shape, BF16),
        dma((2, chunks, TOKENS // CUT)),
        dma((2, chunks, TOKENS // CUT)),
        dma((2, chunks, TOKENS // CUT)),
        dma((2, chunks, TOKENS // CUT)),
        dma((2, REACH)),
        dma((2, REACH)),
        dma((KV, REACH)),
        dma((KV, REACH)),
        dma((TP_SIZE,)),
        dma((TP_SIZE,)),
        dma((2, Z_SIZE)),
        dma((2, Z_SIZE)),
        dma((2, X_SIZE * CORES)),
        dma((2, X_SIZE * CORES)),
        dma((10,)),
        dma((3,)),
    ]
    shapes = (
        wide, wide, jax.ShapeDtypeStruct((n_heads, TOKENS), F32), narrow, narrow, head_row,
        head_row, jax.ShapeDtypeStruct((1, channels), F32), wide, narrow, narrow,
    )
    results = pl.pallas_call(
        kernel,
        out_shape=shapes,
        in_specs=[smem] + [hbm] * 5 + [vmem] * 4 + [hbm] * 5,
        out_specs=(hbm, hbm) + (vmem,) * 6 + (hbm, vmem, vmem),
        scratch_shapes=scratch,
        compiler_params=pltpu.CompilerParams(
            collective_id=0, has_side_effects=True, vmem_limit_bytes=VMEM_LIMIT
        ),
        name="mixer_and_attention",
    )(
        doc_lengths,
        ssm_input[0],
        ssm_gate[0],
        step_raw[0],
        b_proj[0],
        c_proj[0],
        rate_log[None],
        step_bias[None],
        skip_gain[None],
        norm_gain[None],
        ssm_grad_out[0],
        queries[0],
        keys[0],
        values[0],
        attention_output_gradient[0],
    )
    results = pl.pallas_call(
        hand_over,
        out_shape=shapes,
        in_specs=[anywhere] * 11,
        out_specs=(anywhere,) * 11,
        scratch_shapes=[pltpu.VMEM(a.shape, a.dtype) for a in shapes] + [dma((11,)), dma((11,))],
        compiler_params=pltpu.CompilerParams(vmem_limit_bytes=VMEM_LIMIT),
        name="hand_over",
    )(*results)
    gx, ggate, graw, gb, gc, grate, gskip, ggain, gq, gk, gv = results
    return (
        gx[None], ggate[None], graw[None], gb[None], gc[None],
        grate[0], gskip[0], ggain[0], gq[None], gk[None], gv[None],
    )


def solution(mesh):
    tokens = P("dp", "ctx", "tp")
    steps = P("dp", "tp", "ctx")
    param = P("tp")
    return jax.shard_map(
        per_device,
        mesh=mesh,
        in_specs=(
            tokens, tokens, steps, tokens, tokens, param, param, param, param,
            tokens, tokens, tokens, tokens, tokens, P("dp", None),
        ),
        out_specs=(
            tokens, tokens, steps, tokens, tokens, param, param, param,
            tokens, tokens, tokens,
        ),
        check_vma=False,
    )
```
